32 devices in a mesh: tm: 8 (over y, x, core), fsdp: 4 (over z).
Axes of the slice: x: 2, y: 2, z: 4, core: 2. Of those that a mesh axis runs over, the one named last changes fastest.
Arguments:
- frames: bfloat16 [4, 1024, 1024], P('fsdp', 'tm'), may hold values from -6 to 6
- gain_one: float32 [1024], replicated, may hold values from 0.1 to 1.9
- qkv_one: bfloat16 [1024, 3072], P('fsdp'), may hold values from -0.1875 to 0.1875
- out_one: bfloat16 [1024, 1024], P('fsdp'), may hold values from -0.1875 to 0.1875
- gain_two: float32 [1024], replicated, may hold values from 0.1 to 1.9
- qkv_two: bfloat16 [1024, 3072], P('fsdp'), may hold values from -0.1875 to 0.1875
- lengths: int32 [4], P('fsdp'), may hold values from 512 to 1024, as said below
- left_counts: int32 [4], P('fsdp'), may hold values from 0 to 2, as said below
- cotangent: bfloat16 [4, 1024, 1024], P('fsdp', 'tm'), may hold values from -6 to 6
Outputs:
- context: bfloat16 [4, 1024, 1024], P('fsdp', 'tm')
- weight_grad: float32 [1024, 1024], P(('tm', 'fsdp'))
The draws below stay inside these ranges and needn't reach their ends.
Inputs may be any that keep to these rules, and one draw needn't show every extreme that they name: `lengths`: some utterance is complete in every draw. `left_counts`: in every draw some utterance takes 2 blocks and another none.
All inputs are finite; a program needn't handle non-finite values.
Results may differ from the reference program's by a relative error of at most 0.029.
Values may be sent and summed in bfloat16 or wider, within the bound.
A program may use at most 64 MiB of HBM per device.

```python
import jax
import jax.numpy as jnp
from jax import lax

D = 1024
HEADS = 16
HEAD = 64
FR = 128
LEFT_MAX = 2
RIGHT = 23
UTTS = 4
FRAMES = 1024
N_TM = 8


def draw_frames(key, part):
    noise = jax.random.truncated_normal(jax.random.fold_in(key, 31), -6.0, 6.0, (UTTS, FRAMES, D), jnp.float32)
    return noise.astype(jnp.bfloat16)


def projection_draw(key, salt):
    scale = D ** (-0.5)
    base = jax.random.truncated_normal(jax.random.fold_in(key, salt), -6.0, 6.0, (D, 3 * D), jnp.float32) * scale
    return base.astype(jnp.bfloat16)


def draw_qkv_one(key, part):
    return projection_draw(key, 41)


def draw_qkv_two(key, part):
    return projection_draw(key, 51)


def draw_lengths(key, part):
    first = jax.random.fold_in(key, 11)
    second = jax.random.fold_in(key, 12)
    values = jax.random.randint(first, (UTTS,), FRAMES // 2, FRAMES + 1, dtype=jnp.int32)
    chosen = jax.random.randint(second, (), 0, UTTS, dtype=jnp.int32)
    return jnp.where(jnp.arange(UTTS, dtype=jnp.int32) == chosen, FRAMES, values).astype(jnp.int32)


def draw_left_counts(key, part):
    first = jax.random.fold_in(key, 21)
    second = jax.random.fold_in(key, 22)
    third = jax.random.fold_in(key, 23)
    values = jax.random.randint(first, (UTTS,), 0, LEFT_MAX + 1, dtype=jnp.int32)
    chosen = jax.random.randint(second, (), 0, UTTS, dtype=jnp.int32)
    offset = jax.random.randint(third, (), 1, UTTS, dtype=jnp.int32)
    other = (chosen + offset) % UTTS
    index = jnp.arange(UTTS, dtype=jnp.int32)
    values = jnp.where(index == chosen, LEFT_MAX, values)
    values = jnp.where(index == other, 0, values)
    return values.astype(jnp.int32)


def with_spikes(entries, own_key, source, target, parts, factor):
    def block_of(axis_at):
        return (jnp.arange(entries.shape[axis_at]) // (entries.shape[axis_at] // parts)).reshape((-1,) + (1,) * (entries.ndim - 1 - axis_at))

    near = jax.random.permutation(own_key, parts)[block_of(target)]
    other_side = (block_of(target) + parts // 2) % parts
    return jnp.where((block_of(source) == near) | (block_of(source) == other_side), factor * entries, entries)


def block_levels(stream_key, shape, shards, smallest, high):
    loudness, own = 1.0, jax.random.fold_in(stream_key, 6)
    for dim, blocks in shards:
        heights = jnp.exp(jax.random.uniform(jax.random.fold_in(own, dim), (blocks,), jnp.float32, smallest / len(shards), high / len(shards)))
        loudness = loudness * jnp.repeat(heights, shape[dim] // blocks).reshape([-1 if axis == dim else 1 for axis in range(len(shape))])
    return loudness


def gaussian(rng, shape, spread, limit, shards=(), kind=jnp.bfloat16):
    values = spread * jax.random.normal(rng, shape, jnp.float32)
    if shards:
        values = values * block_levels(rng, shape, shards, -0.22, 0.18)
    return jnp.clip(values, -limit, limit).astype(kind)


def bell_draw_with(stream_key, dims, scale, bound, shards, heavy, held_as=jnp.bfloat16):
    result = scale * jax.random.normal(stream_key, dims, jnp.float32)
    if shards:
        result = result * block_levels(stream_key, dims, shards, -0.22, 0.18)
    return jnp.clip(with_spikes(result, jax.random.fold_in(stream_key, 3), *heavy), -bound, bound).astype(held_as)


def setup_inputs(seed: int = 0) -> dict:
    key_of = jax.random.split(jax.random.key(seed), 10)
    frames = draw_frames(jax.random.fold_in(key_of[9], 71), 0)
    gain_one = jnp.clip(1.0 + 0.18 * jax.random.normal(key_of[1], (D,), jnp.float32), 0.1, 1.9)
    qkv_one = draw_qkv_one(jax.random.fold_in(key_of[9], 71), 0)
    out_one = gaussian(key_of[3], (D, D), D ** -0.5, 0.1875, ((0, 4),))
    gain_two = jnp.clip(1.0 + 0.18 * jax.random.normal(key_of[4], (D,), jnp.float32), 0.1, 1.9)
    qkv_two = draw_qkv_two(jax.random.fold_in(key_of[9], 71), 0)
    lengths = draw_lengths(jax.random.fold_in(key_of[9], 71), 0)
    left_counts = draw_left_counts(jax.random.fold_in(key_of[9], 71), 0)
    cotangent = bell_draw_with(key_of[8], (UTTS, FRAMES, D), 1.0, 6.0, ((0, 4), (1, 8)), (1, 2, 8, 2.0))
    return dict(frames=frames, gain_one=gain_one, qkv_one=qkv_one, out_one=out_one, gain_two=gain_two, qkv_two=qkv_two, lengths=lengths, left_counts=left_counts, cotangent=cotangent)


def norm_rows(values, gain):
    wide = values.astype(jnp.float32)
    mean = lax.optimization_barrier(jnp.mean(wide, axis=-1, keepdims=True))
    var = lax.optimization_barrier(jnp.mean((wide - mean) ** 2, axis=-1, keepdims=True))
    return ((wide - mean) * lax.rsqrt(var + 1e-05) * gain.astype(jnp.float32)).astype(jnp.bfloat16)

def attend(query, keys, values, allowed):
    scale = 1.0 / HEAD ** 0.5
    scores = jnp.einsum('qhe,khe->hqk', query.astype(jnp.float32), keys.astype(jnp.float32)) * scale
    scores = jnp.where(allowed[None], scores, -1e+30)
    top = lax.optimization_barrier(jnp.max(scores, axis=-1, keepdims=True))
    expo = jnp.exp(scores - top)
    weights = (expo / lax.optimization_barrier(jnp.sum(expo, axis=-1, keepdims=True))).astype(jnp.bfloat16)
    ctx = jnp.einsum('hqk,khe->qhe', weights.astype(jnp.float32), values.astype(jnp.float32))
    return ctx.reshape(query.shape[0], D).astype(jnp.bfloat16)

def one_utterance(frames_u, gain_one, qkv_one, out_one, gain_two, qkv_two, length, count):
    norm_one = norm_rows(frames_u, gain_one)
    proj = jnp.dot(norm_one, qkv_one, preferred_element_type=jnp.float32).astype(jnp.bfloat16)
    query = proj[:, :D].reshape(FRAMES, HEADS, HEAD)
    keys = proj[:, D:2 * D].reshape(FRAMES, HEADS, HEAD)
    values = proj[:, 2 * D:].reshape(FRAMES, HEADS, HEAD)
    lead = jnp.zeros((LEFT_MAX * FR, HEADS, HEAD), jnp.bfloat16)
    keys_pad = jnp.concatenate([lead, keys], axis=0)
    values_pad = jnp.concatenate([lead, values], axis=0)
    rows = jnp.arange(FR, dtype=jnp.int32)
    cols = jnp.arange((LEFT_MAX + 1) * FR, dtype=jnp.int32)

    def causal_block(block):
        start = (block * FR).astype(jnp.int32)
        qblock = lax.dynamic_slice_in_dim(query, start, FR, 0)
        kblock = lax.dynamic_slice_in_dim(keys_pad, start, (LEFT_MAX + 1) * FR, 0)
        vblock = lax.dynamic_slice_in_dim(values_pad, start, (LEFT_MAX + 1) * FR, 0)
        tpos = block * FR + rows[:, None]
        spos = (block - LEFT_MAX) * FR + cols[None, :]
        apart = LEFT_MAX - cols[None, :] // FR
        allowed = (spos >= 0) & (spos <= tpos) & (apart <= count) & ((spos < length) | (spos == tpos))
        return attend(qblock, kblock, vblock, allowed)
    ctx_one = lax.map(causal_block, jnp.arange(N_TM, dtype=jnp.int32)).reshape(FRAMES, D)
    hidden = (frames_u.astype(jnp.float32) + jnp.dot(ctx_one, out_one, preferred_element_type=jnp.float32)).astype(jnp.bfloat16)
    norm_two = norm_rows(hidden, gain_two)
    proj2 = jnp.dot(norm_two, qkv_two, preferred_element_type=jnp.float32).astype(jnp.bfloat16)
    query2 = proj2[:, :D].reshape(FRAMES, HEADS, HEAD)
    tail = jnp.zeros((FR, HEADS, HEAD), jnp.bfloat16)
    keys2 = jnp.concatenate([proj2[:, D:2 * D].reshape(FRAMES, HEADS, HEAD), tail], axis=0)
    values2 = jnp.concatenate([proj2[:, 2 * D:].reshape(FRAMES, HEADS, HEAD), tail], axis=0)
    cols2 = jnp.arange(FR + RIGHT, dtype=jnp.int32)

    def ahead_block(block):
        start = (block * FR).astype(jnp.int32)
        qblock = lax.dynamic_slice_in_dim(query2, start, FR, 0)
        kblock = lax.dynamic_slice_in_dim(keys2, start, FR + RIGHT, 0)
        vblock = lax.dynamic_slice_in_dim(values2, start, FR + RIGHT, 0)
        tpos = block * FR + rows[:, None]
        spos = block * FR + cols2[None, :]
        allowed = (cols2[None, :] <= rows[:, None] + RIGHT) & ((spos < length) | (spos == tpos))
        ctx = attend(qblock, kblock, vblock, allowed)
        valid = block * FR + rows < length
        return jnp.where(valid[:, None], ctx, jnp.zeros_like(ctx))
    return lax.map(ahead_block, jnp.arange(N_TM, dtype=jnp.int32)).reshape(FRAMES, D)

def reference(frames, gain_one, qkv_one, out_one, gain_two, qkv_two, lengths, left_counts, cotangent):

    def per_utt(index):
        return one_utterance(frames[index], gain_one, qkv_one, out_one, gain_two, qkv_two, lengths[index], left_counts[index])
    context = lax.map(per_utt, jnp.arange(UTTS, dtype=jnp.int32))
    weight_grad = jnp.dot(cotangent.reshape(-1, D).T, context.reshape(-1, D), preferred_element_type=jnp.float32)
    return (context, weight_grad)
```

```python
import contextlib
import functools
import math

import jax
import jax.numpy as jnp
from jax import lax
from jax.experimental import pallas as pl
from jax.experimental.pallas import tpu as pltpu
from jax.sharding import PartitionSpec as P

HEADS = 16
LEFT_MAX = 2
RIGHT = 23
CHIPS = 4
SCOPES = False


def mark(name):
    return jax.named_scope(name) if SCOPES else contextlib.nullcontext()


def from_behind(block, axis, distance):
    devices = range(lax.axis_size(axis))
    route = [(i - distance, i) for i in devices if i - distance in devices]
    return lax.ppermute(block, axis, route)


def norm_rows(values, gain):
    wide = values.astype(jnp.float32)
    mean = jnp.mean(wide, axis=-1, keepdims=True)
    var = jnp.mean((wide - mean) ** 2, axis=-1, keepdims=True)
    return ((wide - mean) * lax.rsqrt(var + 1e-05) * gain).astype(jnp.bfloat16)


def attend(query, keys, values, allowed, heads):
    rows_q, width = query.shape
    head = width // heads
    scale = 1.0 / head**0.5
    q_heads = query.reshape(rows_q, heads, head)
    k_heads = keys.reshape(keys.shape[0], heads, head)
    v_heads = values.reshape(values.shape[0], heads, head)
    scores = (
        jnp.einsum("qhe,khe->hqk", q_heads, k_heads, preferred_element_type=jnp.float32) * scale
    )
    scores = jnp.where(allowed[None], scores, -1e30)
    top = jnp.max(scores, axis=-1, keepdims=True)
    expo = jnp.exp(scores - top)
    weights = (expo / jnp.sum(expo, axis=-1, keepdims=True)).astype(jnp.bfloat16)
    ctx = jnp.einsum("hqk,khe->qhe", weights, v_heads, preferred_element_type=jnp.float32)
    return ctx.reshape(rows_q, width).astype(jnp.bfloat16)


def add_rows(left, piece):
    return jnp.dot(left, piece, preferred_element_type=jnp.float32)


def on_device(
    frames, gain_one, qkv_one, out_one, gain_two, qkv_two, lengths, left_counts, cotangent
):
    local = frames[0]
    grad_in = cotangent[0]
    fr, width = local.shape
    block = lax.axis_index("tm")
    length = lengths[0]
    count = left_counts[0]
    norm_one = norm_rows(local, gain_one)
    proj = add_rows(norm_one, lax.all_gather(qkv_one, "fsdp", axis=0, tiled=True))
    proj = proj.astype(jnp.bfloat16)
    query = proj[:, :width]
    key_value = proj[:, width:]
    earlier = [from_behind(key_value, "tm", step) for step in range(LEFT_MAX, 0, -1)]
    gathered = jnp.concatenate(earlier + [key_value], axis=0)
    rows = jnp.arange(fr, dtype=jnp.int32)
    cols = jnp.arange((LEFT_MAX + 1) * fr, dtype=jnp.int32)
    tpos = block * fr + rows[:, None]
    spos = (block - LEFT_MAX) * fr + cols[None, :]
    apart = LEFT_MAX - cols[None, :] // fr
    allowed = (spos >= 0) & (spos <= tpos) & (apart <= count) & ((spos < length) | (spos == tpos))
    ctx_one = attend(query, gathered[:, :width], gathered[:, width:], allowed, HEADS)
    out_proj = add_rows(ctx_one, lax.all_gather(out_one, "fsdp", axis=0, tiled=True))
    hidden = (local.astype(jnp.float32) + out_proj).astype(jnp.bfloat16)
    norm_two = norm_rows(hidden, gain_two)
    proj2 = add_rows(norm_two, lax.all_gather(qkv_two, "fsdp", axis=0, tiled=True))
    proj2 = proj2.astype(jnp.bfloat16)
    query2 = proj2[:, :width]
    key_value2 = proj2[:, width:]
    ahead = from_behind(key_value2[:RIGHT], "tm", -1)
    joined = jnp.concatenate([key_value2, ahead], axis=0)
    cols2 = jnp.arange(fr + RIGHT, dtype=jnp.int32)
    spos2 = block * fr + cols2[None, :]
    allowed2 = (cols2[None, :] <= rows[:, None] + RIGHT) & ((spos2 < length) | (spos2 == tpos))
    ctx_two = attend(query2, joined[:, :width], joined[:, width:], allowed2, HEADS)
    valid = block * fr + rows < length
    context = jnp.where(valid[:, None], ctx_two, jnp.zeros_like(ctx_two))
    weight_grad = lax.psum_scatter(
        lax.dot_general(
            grad_in, context, (((0,), (0,)), ((), ())), preferred_element_type=jnp.float32
        ),
        ("tm", "fsdp"),
        scatter_dimension=0,
        tiled=True,
    )
    return (context[None], weight_grad)


MESH = pl.DeviceIdType.MESH


def flip(index, mask):
    out, bit = index, 1
    while bit <= mask:
        if mask & bit:
            out = out + bit * (1 - 2 * ((index // bit) % 2))
        bit *= 2
    return out


def heads_kernel(
    n,
    nz,
    frames_ref, gain_one_ref, qkv_one_ref, out_one_ref, gain_two_ref, qkv_two_ref,
    length_ref, count_ref, cot_ref,
    context_ref, grad_ref,
    fbuf, nbuf, nbuf2, w1, w2, wo, cotv, cott, gains,
    q1, k1a, k1b, v1a, v1b, p1, r1, ctx1s, ctxall,
    q2, k2a, k2b, v2a, v2b, p2, pn2, r2, ctx2s, ctx2,
    gsend, grecv, gsum, wgr,
    local_sem, ag_send, ag_recv, ch_send, ch_recv, cx_send, cx_recv, nx_send, nx_recv,
    a2_send, a2_recv, z_send, z_recv,
):
    t = lax.axis_index("tm")
    z = lax.axis_index("fsdp")
    fr, width = frames_ref.shape
    cols = width // n
    head = width // HEADS
    per = HEADS // n
    rows = width // nz
    part = rows // n
    groups = n // 2
    scale = math.log2(math.e) / head**0.5
    mine = pl.multiple_of(t * cols, cols)
    core = lax.rem(t, 2)

    def at_cols(index):
        return pl.ds(pl.multiple_of(index * cols, cols), cols)

    def at_rows(index, size):
        return pl.ds(pl.multiple_of(index * size, size), size)

    barrier = pltpu.get_barrier_semaphore()
    for mask in (4, 2, 1):
        pl.semaphore_signal(barrier, inc=1, device_id=(flip(t, mask), z), device_id_type=MESH)

    @pl.when(z > 0)
    def _():
        pl.semaphore_signal(barrier, inc=1, device_id=(t, z - 1), device_id_type=MESH)

    @pl.when(z < nz - 1)
    def _():
        pl.semaphore_signal(barrier, inc=1, device_id=(t, z + 1), device_id_type=MESH)

    own_rows = at_rows(z, rows)

    def load(src, dst, index):
        return pltpu.make_async_copy(src, dst, local_sem.at[index])

    def load_cols(src, dst, j, index):
        return load(
            src.at[:, pl.ds(pl.multiple_of(j * width + mine, cols), cols)],
            dst.at[own_rows, pl.ds(j * cols, cols)],
            index,
        )

    get_frames = load(frames_ref, fbuf.at[t], 0)
    get_wo = load(out_one_ref, wo.at[pl.ds(0, rows), :], 1)
    get_w1 = [load_cols(qkv_one_ref, w1, j, 2 + j) for j in range(3)]
    get_w2 = [load_cols(qkv_two_ref, w2, j, 5 + j) for j in range(3)]
    get_cot = load(cot_ref, cotv, 8)
    get_gains = [load(gain_one_ref, gains.at[0:1], 9), load(gain_two_ref, gains.at[1:2], 10)]
    for copy in [get_frames, get_wo, *get_w1, *get_gains, get_cot, *get_w2]:
        copy.start()

    half = rows // 2

    def chain_view(which, shard, h, at):
        place = lax.rem(shard - at + nz, nz) if which == 0 else shard
        span = pl.ds(pl.multiple_of(place * rows + h * half, half), half)
        if which == 0:
            return wo.at[span, pl.ds(mine, cols)]
        wide = pl.ds(0, 2 * cols) if which in (1, 3) else pl.ds(2 * cols, cols)
        return (w1 if which < 3 else w2).at[span, wide]

    def chain_copy(which, step, up, h):
        shard = z - step if up else z + step
        shard = jnp.clip(shard, 0, nz - 1)
        to = jnp.clip(z + 1 if up else z - 1, 0, nz - 1)
        return pltpu.make_async_remote_copy(
            src_ref=chain_view(which, shard, h, z),
            dst_ref=chain_view(which, shard, h, to),
            send_sem=ch_send.at[which, 0 if up else 1, step, h],
            recv_sem=ch_recv.at[which, shard, h],
            device_id=(t, to),
            device_id_type=MESH,
        )

    def chain_wait(which, shard, h, other):
        view = chain_view(which, shard, h, z)
        pltpu.make_async_remote_copy(
            src_ref=view,
            dst_ref=view,
            send_sem=ch_send.at[which, 0, 0, h],
            recv_sem=ch_recv.at[which, shard, h],
            device_id=(t, other),
            device_id_type=MESH,
        ).wait_recv()

    def chain_cond(step, up):
        if up:
            return (z >= step) & (z < nz - 1)
        return (z + step < nz) & (z > 0)

    def chain(which, step, halves=(0, 1)):
        for h in halves:
            for up in (True, False):
                @pl.when(chain_cond(step, up))
                def _():
                    copy = chain_copy(which, step, up, h)
                    if step:
                        chain_wait(which, z - step if up else z + step, h, z + 1 if up else z - 1)
                    copy.start()

    def chain_end(which):
        for edge, up in ((nz - 1, True), (0, False)):
            @pl.when(z == edge)
            def _():
                for step in range(1, nz):
                    for h in range(2):
                        shard = edge - step if up else edge + step
                        chain_wait(which, shard, h, edge - 1 if up else edge + 1)

    def chain_sent(which):
        for step in range(nz - 1):
            for up in (True, False):
                for h in range(2):
                    @pl.when(chain_cond(step, up))
                    def _():
                        chain_copy(which, step, up, h).wait_send()

    def ag_view(which, index, piece):
        if which == 0:
            if piece is None:
                return fbuf.at[index]
            return fbuf.at[index, pl.ds(piece * (fr // 2), fr // 2), :]
        buf, first, size = (
            None, (cott, 0, width // 2), (wo, rows, width - rows), (cott, width // 2, width // 2),
        )[which]
        if piece is None:
            return buf.at[pl.ds(first, size), at_cols(index)]
        return buf.at[pl.ds(first + piece * (size // 2), size // 2), at_cols(index)]

    slots = (
        (0, None, 1), (0, 0, 2), (0, 1, 2), (0, 1, 4), (0, 0, 4),
        (2, 0, 4), (4, 1, 2),
        (2, None, 1), (4, None, 1), (6, 0, 1), (6, 1, 1),
    )

    def ag_copy(which, slot):
        block, piece, to = slots[slot]
        view = ag_view(which, flip(t, block), piece)
        return pltpu.make_async_remote_copy(
            src_ref=view, dst_ref=view,
            send_sem=ag_send.at[which, slot], recv_sem=ag_recv.at[which, slot],
            device_id=(flip(t, to), z), device_id_type=MESH,
        )

    def ag_wait(which, slot):
        block, piece, to = slots[slot]
        view = ag_view(which, flip(t, block ^ to), piece)
        pltpu.make_async_remote_copy(
            src_ref=view, dst_ref=view,
            send_sem=ag_send.at[which, slot], recv_sem=ag_recv.at[which, slot],
            device_id=(flip(t, to), z), device_id_type=MESH,
        ).wait_recv()

    def ag_start(which):
        for slot in (1, 3, 2, 4, 0):
            ag_copy(which, slot).start()

    def ag_forward(which, stage):
        for waits, slot in (
            (((1, 5), (3, 6)), ((2, 7), (4, 8)), ((5, 9), (6, 10)))[stage]
        ):
            ag_wait(which, waits)
            ag_copy(which, slot).start()

    def ag_partner(which):
        for slot in (0, 7, 8, 9, 10):
            ag_wait(which, slot)

    def ag_sent(which):
        for slot in range(len(slots)):
            ag_copy(which, slot).wait_send()

    def normed(index):
        nbuf[index] = norm_rows(fbuf[index], gains[0:1, :])

    def masked_heads(values):
        lane = lax.broadcasted_iota(jnp.int32, values.shape, 1) // head
        blank = jnp.zeros_like(values)
        return jnp.where(lane == 0, values, blank), jnp.where(lane == 1, values, blank)

    def dot(left, right):
        return jnp.dot(left, right, preferred_element_type=jnp.float32)

    def dot_t(left, right):
        return lax.dot_general(
            left, right, (((1,), (1,)), ((), ())), preferred_element_type=jnp.float32
        )

    def project(buf, weight, pair, targets_qk, targets_v):
        left = buf[2 * pair : 2 * pair + 2].reshape(2 * fr, width)
        span = pl.ds(2 * pair * fr, 2 * fr)
        if targets_qk is not None:
            q, ka, kb = targets_qk
            out = dot(left, weight[:, : 2 * cols]).astype(jnp.bfloat16)
            q[span, :] = out[:, :cols]
            ka[span, :], kb[span, :] = masked_heads(out[:, cols:])
        else:
            va, vb = targets_v
            out = dot(left, weight[:, 2 * cols :]).astype(jnp.bfloat16)
            va[span, :], vb[span, :] = masked_heads(out)

    def turned(index):
        return lax.rem(index - z * (rows // cols) + n, n)

    with mark("a_barrier"):
        pl.semaphore_wait(
            barrier, 3 + jnp.where(z > 0, 1, 0) + jnp.where(z < nz - 1, 1, 0)
        )
    with mark("b_frames"):
        get_frames.wait()
    ag_start(0)
    get_wo.wait()
    chain(0, 0)
    with mark("c_w1local"):
        get_w1[0].wait()
        get_w1[1].wait()
    chain(1, 0, (0,))
    with mark("d_norm"):
        for copy in get_gains:
            copy.wait()
        normed(t)
    with mark("e_chain01"):
        chain(0, 1)
    chain(1, 0, (1,))
    with mark("f_agf00"):
        ag_forward(0, 0)
    with mark("g_turn"):
        get_cot.wait()
        turned_cot = cotv[...].T
        for zz in range(nz):
            for tt in range(n):
                cott[zz * rows + tt * part : zz * rows + (tt + 1) * part, pl.ds(mine, cols)] = (
                    turned_cot[(tt * nz + zz) * part : (tt * nz + zz + 1) * part]
                )
        ag_wait(0, 0)
        normed(flip(t, 1))
    with mark("h_chain02"):
        chain(0, 2)
    with mark("i_agf01"):
        ag_forward(0, 1)
    with mark("j_chain11"):
        chain(1, 1)
    with mark("k_chainend0"):
        chain_end(0)
    ag_start(2)
    with mark("l_norms"):
        normed(flip(t, 2))
        normed(flip(t, 4))
    with mark("m_chain12"):
        chain(1, 2)
    get_w1[2].wait()
    chain(2, 0)
    with mark("n_agf02"):
        ag_forward(0, 2)
    with mark("o_norms"):
        ag_wait(0, 7)
        normed(flip(t, 3))
        ag_wait(0, 8)
        normed(flip(t, 5))
        normed(flip(t, 6))
    with mark("p_agf20"):
        ag_forward(2, 0)
    with mark("q_norm"):
        ag_wait(0, 9)
        ag_wait(0, 10)
        normed(flip(t, 7))
    with mark("r_chainend1"):
        chain_end(1)
    with mark("s_projqk"):
        for pair in range(groups):
            project(nbuf, w1, pair, (q1, k1a, k1b), None)

    length = length_ref[0]
    count = count_ref[0]
    row = lax.broadcasted_iota(jnp.int32, (fr, fr), 0)
    col = lax.broadcasted_iota(jnp.int32, (fr, fr), 1)
    low = -1e30

    def spans(b):
        first = max(b - LEFT_MAX, 0)
        return pl.ds(first * fr, (b + 1 - first) * fr), b - first

    def causal(b):
        span, before = spans(b)
        size = (before + 1) * fr
        query = q1[b * fr : (b + 1) * fr, :]
        both = dot_t(query, jnp.concatenate([k1a[span, :], k1b[span, :]], axis=0))
        spos = (b - before) * fr + lax.broadcasted_iota(jnp.int32, (1, size), 1)
        apart = before - lax.broadcasted_iota(jnp.int32, (1, size), 1) // fr
        bias = jnp.where((apart <= count) & (spos < length), 0.0, low)
        expos, inverse = [], []
        for h in range(per):
            scores = both[:, h * size : (h + 1) * size]
            now = scores[:, before * fr :]
            now = jnp.where(
                row > col,
                now + bias[:, before * fr :],
                jnp.where(row == col, now, low),
            )
            if before:
                now = jnp.concatenate(
                    [scores[:, : before * fr] + bias[:, : before * fr], now], axis=1
                )
            top = jnp.max(now, axis=-1, keepdims=True)
            expo = jnp.exp2((now - top) * scale)
            inverse.append(1.0 / jnp.sum(expo, axis=-1, keepdims=True))
            expos.append(expo.astype(jnp.bfloat16))
        p1[b, :, : per * size] = jnp.concatenate(expos, axis=1)
        r1[b] = jnp.where(col // head == 0, inverse[0], inverse[1])

    def causal_mix(b):
        span, before = spans(b)
        size = (before + 1) * fr
        mixed = dot(
            p1[b, :, : per * size], jnp.concatenate([v1a[span, :], v1b[span, :]], axis=0)
        )
        ctx1s[b * fr : (b + 1) * fr, :] = (mixed * r1[b]).astype(jnp.bfloat16)

    with mark("t_soft0"):
        causal(0)
        causal(1)
    with mark("ta_chain21"):
        chain(2, 1)
    with mark("tb_agf21"):
        ag_forward(2, 1)
    with mark("t_soft1"):
        causal(2)
        causal(3)
    with mark("tc_chain22"):
        chain(2, 2, (0,))
    with mark("td_agf22"):
        ag_forward(2, 2)
    ag_start(1)
    with mark("t_soft2"):
        causal(4)
        causal(5)
    with mark("te_chain22"):
        chain(2, 2, (1,))
    for copy in get_w2:
        copy.wait()
    chain(3, 0)
    with mark("t_soft3"):
        causal(6)
        causal(7)
    with mark("u_agf10"):
        ag_forward(1, 0)
    with mark("v_chainend2"):
        chain_end(2)
    with mark("w_projv"):
        for pair in range(groups):
            project(nbuf, w1, pair, None, (v1a, v1b))

    def cx_copy(g, m):
        to = flip(t, (m, 4, 2)[max(m - 5, 0)])
        if m < 6:
            src = ctx1s.at[at_rows(2 * g + lax.rem(core + m, 2), fr), :]
            dst = ctxall.at[g, :, at_cols(turned(t))]
        else:
            first = turned(flip(t, 2 if m == 6 else 4) // 2 * 2)
            src = ctxall.at[
                g,
                pl.ds((m - 6) * (fr // 2), fr // 2),
                pl.ds(pl.multiple_of(first * cols, 2 * cols), 2 * cols),
            ]
            dst = src
        return pltpu.make_async_remote_copy(
            src_ref=src, dst_ref=dst,
            send_sem=cx_send.at[g, m], recv_sem=cx_recv.at[g, m],
            device_id=(to, z), device_id_type=MESH,
        )

    def cx_wait(g, m):
        to = flip(t, (m, 4, 2)[max(m - 5, 0)])
        if m < 6:
            view = ctxall.at[g, :, at_cols(turned(to))]
        else:
            view = ctxall.at[
                g,
                pl.ds((m - 6) * (fr // 2), fr // 2),
                pl.ds(pl.multiple_of(turned(flip(t, 6) // 2 * 2) * cols, 2 * cols), 2 * cols),
            ]
        pltpu.make_async_remote_copy(
            src_ref=view, dst_ref=view,
            send_sem=cx_send.at[g, m], recv_sem=cx_recv.at[g, m],
            device_id=(to, z), device_id_type=MESH,
        ).wait_recv()

    def cx_forward(g):
        cx_wait(g, 2)
        cx_wait(g, 3)
        cx_copy(g, 6).start()
        cx_wait(g, 4)
        cx_wait(g, 5)
        cx_copy(g, 7).start()

    with mark("x_mix"):
        for g in range(groups):
            causal_mix(2 * g)
            causal_mix(2 * g + 1)
            for m in (2, 4, 3, 5, 1):
                cx_copy(g, m).start()
            ctxall[g, :, at_cols(turned(t))] = ctx1s[at_rows(2 * g + core, fr), :]
    with mark("xa_agf11"):
        ag_forward(1, 1)
    with mark("xb_chain31"):
        chain(3, 1)
    with mark("xc_agf12"):
        ag_forward(1, 2)
    with mark("xd_fwd0"):
        cx_forward(0)
    with mark("xe_agp2"):
        ag_partner(2)
    with mark("xf_fwd1"):
        cx_forward(1)
    with mark("xg_chain32"):
        chain(3, 2)
    chain(4, 0)
    with mark("xh_fwd2"):
        cx_forward(2)
    with mark("xi_fwd3"):
        cx_forward(3)
    ag_start(3)
    with mark("xj_agp1"):
        ag_partner(1)

    def nx_copy(g, other):
        view = nbuf2.at[2 * g + (1 - core if other else core)]
        return pltpu.make_async_remote_copy(
            src_ref=view, dst_ref=view,
            send_sem=nx_send.at[g], recv_sem=nx_recv.at[g],
            device_id=(flip(t, 1), z), device_id_type=MESH,
        )

    def out_block(g):
        for m in (1, 6, 7):
            cx_wait(g, m)
        b = 2 * g + core
        mixed = dot(ctxall[g], wo[...])
        hidden = (fbuf[b].astype(jnp.float32) + mixed).astype(jnp.bfloat16)
        nbuf2[b] = norm_rows(hidden, gains[1:2, :])
        nx_copy(g, False).start()

    tail = -(-RIGHT // 16) * 16
    wide = lax.broadcasted_iota(jnp.int32, (tail, tail), 1)
    long = lax.broadcasted_iota(jnp.int32, (tail, tail), 0) + (fr - tail)

    def ahead(b):
        query = q2[b * fr : (b + 1) * fr, :]
        here = pl.ds(b * fr, fr)
        both = dot_t(query, jnp.concatenate([k2a[here, :], k2b[here, :]], axis=0))
        seen = jnp.where(b * fr + lax.broadcasted_iota(jnp.int32, (1, fr), 1) < length, 0.0, low)
        after = None
        if b < n - 1:
            there = pl.ds((b + 1) * fr, tail)
            after = dot_t(
                query[fr - tail :], jnp.concatenate([k2a[there, :], k2b[there, :]], axis=0)
            )
            spos = (b + 1) * fr + lax.broadcasted_iota(jnp.int32, (1, tail), 1)
            late = jnp.where(spos < length, 0.0, low)
        expos, lates, inverse = [], [], []
        for h in range(per):
            now = both[:, h * fr : (h + 1) * fr]
            now = jnp.where(
                row == col, now, jnp.where(col <= row + RIGHT, now + seen, low)
            )
            top = jnp.max(now, axis=-1, keepdims=True)
            if after is not None:
                then = after[:, h * tail : (h + 1) * tail]
                then = jnp.where(wide + fr <= long + RIGHT, then + late, low)
                top = jnp.concatenate(
                    [
                        top[: fr - tail],
                        jnp.maximum(top[fr - tail :], jnp.max(then, axis=-1, keepdims=True)),
                    ],
                    axis=0,
                )
            expo = jnp.exp2((now - top) * scale)
            total = jnp.sum(expo, axis=-1, keepdims=True)
            if after is not None:
                then = jnp.exp2((then - top[fr - tail :]) * scale)
                total = jnp.concatenate(
                    [
                        total[: fr - tail],
                        total[fr - tail :] + jnp.sum(then, axis=-1, keepdims=True),
                    ],
                    axis=0,
                )
                lates.append(then.astype(jnp.bfloat16))
            inverse.append(1.0 / total)
            expos.append(expo.astype(jnp.bfloat16))
        p2[b] = jnp.concatenate(expos, axis=1)
        if after is not None:
            pn2[b] = jnp.concatenate(lates, axis=1)
        valid = b * fr + row < length
        r2[b] = jnp.where(valid, jnp.where(col // head == 0, inverse[0], inverse[1]), 0.0)

    def ahead_mix(b):
        here = pl.ds(b * fr, fr)
        mixed = dot(p2[b], jnp.concatenate([v2a[here, :], v2b[here, :]], axis=0))
        if b < n - 1:
            there = pl.ds((b + 1) * fr, tail)
            extra = dot(pn2[b], jnp.concatenate([v2a[there, :], v2b[there, :]], axis=0))
            mixed = jnp.concatenate([mixed[: fr - tail], mixed[fr - tail :] + extra], axis=0)
        ctx2s[b * fr : (b + 1) * fr, :] = (mixed * r2[b]).astype(jnp.bfloat16)

    with mark("y_out0"):
        out_block(0)
    with mark("y_out1"):
        out_block(1)
    with mark("ya_chain41"):
        chain(4, 1)
    with mark("y_out2"):
        out_block(2)
    with mark("y_out3"):
        out_block(3)
    with mark("yb_agf30"):
        ag_forward(3, 0)
    with mark("yc_chainend3"):
        chain_end(3)
    for g in range(groups):
        with mark(f"yd_proj{g}"):
            nx_copy(g, True).wait_recv()
            project(nbuf2, w2, g, (q2, k2a, k2b), None)
            if g:
                ahead(2 * g - 1)
            ahead(2 * g)
        if g == 1:
            with mark("ye_agf31"):
                ag_forward(3, 1)
        if g == 2:
            with mark("yf_chain42"):
                chain(4, 2)
    with mark("yg_last"):
        ahead(n - 1)
    with mark("yh_agf32"):
        ag_forward(3, 2)
    with mark("yi_chainend4"):
        chain_end(4)
    with mark("yj_mix2"):
        for g in range(groups):
            project(nbuf2, w2, g, None, (v2a, v2b))
        for b in range(n):
            ahead_mix(b)
    with mark("yk_agp3"):
        ag_partner(3)

    def back_copy(d):
        b = lax.rem(t + d, n)
        return pltpu.make_async_remote_copy(
            src_ref=ctx2s.at[at_rows(b, fr), :],
            dst_ref=ctx2.at[:, at_cols(t)],
            send_sem=a2_send.at[0, d], recv_sem=a2_recv.at[0, d],
            device_id=(b, z), device_id_type=MESH,
        )

    def back_wait(d):
        b = lax.rem(t + n - d, n)
        pltpu.make_async_remote_copy(
            src_ref=ctx2s.at[at_rows(b, fr), :],
            dst_ref=ctx2.at[:, at_cols(b)],
            send_sem=a2_send.at[0, d], recv_sem=a2_recv.at[0, d],
            device_id=(b, z), device_id_type=MESH,
        ).wait_recv()

    def term(zz):
        return dot(cott[at_rows(zz, rows), :], ctx2s[...])

    def z_copy(d):
        to = lax.rem(z + d, nz)
        return pltpu.make_async_remote_copy(
            src_ref=gsend.at[d], dst_ref=grecv.at[d],
            send_sem=z_send.at[d], recv_sem=z_recv.at[d],
            device_id=(t, to), device_id_type=MESH,
        )

    with mark("z_terms"):
        for d in range(1, nz):
            gsend[d] = term(lax.rem(z + d, nz)).astype(jnp.bfloat16)
            z_copy(d).start()
        for d in range(1, n):
            back_copy(d).start()
        ctx2[:, at_cols(t)] = ctx2s[at_rows(t, fr), :]
        total = term(z)
    with mark("za_zwait"):
        for d in range(1, nz):
            z_copy(d).wait_recv()
            total = total + grecv[d].astype(jnp.float32)
        gsum[...] = total

    def g_copy(d):
        b = lax.rem(t + d, n)
        return pltpu.make_async_remote_copy(
            src_ref=gsum.at[at_rows(b, part), :],
            dst_ref=wgr.at[:, pl.ds(mine, cols)],
            send_sem=a2_send.at[1, d], recv_sem=a2_recv.at[1, d],
            device_id=(b, z), device_id_type=MESH,
        )

    for d in range(1, n):
        g_copy(d).start()
    with mark("zb_back"):
        wgr[:, pl.ds(mine, cols)] = gsum[at_rows(t, part), :]
        for d in range(1, n):
            back_wait(d)
        context_ref[...] = ctx2[...]
    with mark("zc_gwait"):
        for d in range(1, n):
            b = lax.rem(t + n - d, n)
            pltpu.make_async_remote_copy(
                src_ref=gsum.at[at_rows(b, part), :],
                dst_ref=wgr.at[:, at_cols(b)],
                send_sem=a2_send.at[1, d], recv_sem=a2_recv.at[1, d],
                device_id=(b, z), device_id_type=MESH,
            ).wait_recv()
        grad_ref[...] = wgr[...]
    with mark("zd_sent"):
        for which in range(4):
            ag_sent(which)
        for which in range(5):
            chain_sent(which)
        for g in range(groups):
            nx_copy(g, False).wait_send()
            for m in range(1, 8):
                cx_copy(g, m).wait_send()
        for d in range(1, n):
            back_copy(d).wait_send()
            g_copy(d).wait_send()
        for d in range(1, nz):
            z_copy(d).wait_send()


def hand_out(context_ref, grad_ref, context_out, grad_out):
    context_out[...] = context_ref[...]
    grad_out[...] = grad_ref[...]


def by_heads(
    n, nz, frames, gain_one, qkv_one, out_one, gain_two, qkv_two, lengths, left_counts, cotangent
):
    _, fr, width = frames.shape
    cols = width // n
    rows = width // nz
    span = n * fr
    tail = -(-RIGHT // 16) * 16
    per = HEADS // n
    vmem = pl.BlockSpec(memory_space=pltpu.VMEM)
    smem = pl.BlockSpec(memory_space=pltpu.SMEM)
    hbm = pl.BlockSpec(memory_space=pltpu.HBM)
    bf16, f32 = jnp.bfloat16, jnp.float32
    dma = pltpu.SemaphoreType.DMA
    large = (
        frames[0], gain_one[None], qkv_one, out_one, gain_two[None], qkv_two, cotangent[0],
    )
    large = [pltpu.with_memory_space_constraint(value, pltpu.HBM) for value in large]
    context, grad = pl.pallas_call(
        functools.partial(heads_kernel, n, nz),
        out_shape=(
            jax.ShapeDtypeStruct((fr, width), bf16),
            jax.ShapeDtypeStruct((rows // n, width), f32),
        ),
        in_specs=[hbm] * 6 + [smem] * 2 + [hbm],
        out_specs=(vmem, vmem),
        scratch_shapes=[
            pltpu.VMEM((n, fr, width), bf16),
            pltpu.VMEM((n, fr, width), bf16),
            pltpu.VMEM((n, fr, width), bf16),
            pltpu.VMEM((width, 3 * cols), bf16),
            pltpu.VMEM((width, 3 * cols), bf16),
            pltpu.VMEM((width, width), bf16),
            pltpu.VMEM((fr, width), bf16),
            pltpu.VMEM((width, span), bf16),
            pltpu.VMEM((2, width), f32),
            *[pltpu.VMEM((span, cols), bf16)] * 5,
            pltpu.VMEM((n, fr, per * (LEFT_MAX + 1) * fr), bf16),
            pltpu.VMEM((n, fr, cols), f32),
            pltpu.VMEM((span, cols), bf16),
            pltpu.VMEM((n // 2, fr, width), bf16),
            *[pltpu.VMEM((span, cols), bf16)] * 5,
            pltpu.VMEM((n, fr, per * fr), bf16),
            pltpu.VMEM((n, tail, per * tail), bf16),
            pltpu.VMEM((n, fr, cols), f32),
            pltpu.VMEM((span, cols), bf16),
            pltpu.VMEM((fr, width), bf16),
            pltpu.VMEM((nz, rows, cols), bf16),
            pltpu.VMEM((nz, rows, cols), bf16),
            pltpu.VMEM((rows, cols), f32),
            pltpu.VMEM((rows // n, width), f32),
            dma((11,)),
            dma((4, 11)),
            dma((4, 11)),
            dma((5, 2, nz, 2)),
            dma((5, nz, 2)),
            dma((n // 2, 8)),
            dma((n // 2, 8)),
            dma((n // 2,)),
            dma((n // 2,)),
            dma((2, n)),
            dma((2, n)),
            dma((nz,)),
            dma((nz,)),
        ],
        compiler_params=pltpu.CompilerParams(
            collective_id=0, has_side_effects=True, vmem_limit_bytes=44 * 1024 * 1024
        ),
    )(*large[:6], lengths, left_counts, large[6])
    context, grad = pl.pallas_call(
        hand_out,
        out_shape=(
            jax.ShapeDtypeStruct((fr, width), bf16),
            jax.ShapeDtypeStruct((rows // n, width), f32),
        ),
        in_specs=[vmem, vmem],
        out_specs=(vmem, vmem),
        compiler_params=pltpu.CompilerParams(vmem_limit_bytes=4 * 1024 * 1024),
    )(context, grad)
    return (context[None], grad)


def solution(mesh):
    n_tm = mesh.shape["tm"]
    even = n_tm == 2 * CHIPS and mesh.shape["fsdp"] == CHIPS and HEADS == 2 * n_tm
    chosen = functools.partial(by_heads, n_tm, mesh.shape["fsdp"]) if even else on_device
    in_specs = (
        P("fsdp", "tm", None),
        P(),
        P("fsdp", None),
        P("fsdp", None),
        P(),
        P("fsdp", None),
        P("fsdp"),
        P("fsdp"),
        P("fsdp", "tm", None),
    )
    out_specs = (P("fsdp", "tm", None), P(("tm", "fsdp"), None))
    return jax.shard_map(
        chosen, mesh=mesh, in_specs=in_specs, out_specs=out_specs, check_vma=False
    )
```

```python
import contextlib
import functools
import math

import jax
import jax.numpy as jnp
from jax import lax
from jax.experimental import pallas as pl
from jax.experimental.pallas import tpu as pltpu
from jax.sharding import PartitionSpec as P

HEADS = 16
LEFT_MAX = 2
RIGHT = 23
CHIPS = 4
SCOPES = False


def mark(name):
    return jax.named_scope(name) if SCOPES else contextlib.nullcontext()


def from_behind(block, axis, distance):
    devices = range(lax.axis_size(axis))
    route = [(i - distance, i) for i in devices if i - distance in devices]
    return lax.ppermute(block, axis, route)


def norm_rows(values, gain):
    wide = values.astype(jnp.float32)
    mean = jnp.mean(wide, axis=-1, keepdims=True)
    var = jnp.mean((wide - mean) ** 2, axis=-1, keepdims=True)
    return ((wide - mean) * lax.rsqrt(var + 1e-05) * gain).astype(jnp.bfloat16)


def attend(query, keys, values, allowed, heads):
    rows_q, width = query.shape
    head = width // heads
    scale = 1.0 / head**0.5
    q_heads = query.reshape(rows_q, heads, head)
    k_heads = keys.reshape(keys.shape[0], heads, head)
    v_heads = values.reshape(values.shape[0], heads, head)
    scores = (
        jnp.einsum("qhe,khe->hqk", q_heads, k_heads, preferred_element_type=jnp.float32) * scale
    )
    scores = jnp.where(allowed[None], scores, -1e30)
    top = jnp.max(scores, axis=-1, keepdims=True)
    expo = jnp.exp(scores - top)
    weights = (expo / jnp.sum(expo, axis=-1, keepdims=True)).astype(jnp.bfloat16)
    ctx = jnp.einsum("hqk,khe->qhe", weights, v_heads, preferred_element_type=jnp.float32)
    return ctx.reshape(rows_q, width).astype(jnp.bfloat16)


def add_rows(left, piece):
    return jnp.dot(left, piece, preferred_element_type=jnp.float32)


def on_device(
    frames, gain_one, qkv_one, out_one, gain_two, qkv_two, lengths, left_counts, cotangent
):
    local = frames[0]
    grad_in = cotangent[0]
    fr, width = local.shape
    block = lax.axis_index("tm")
    length = lengths[0]
    count = left_counts[0]
    norm_one = norm_rows(local, gain_one)
    proj = add_rows(norm_one, lax.all_gather(qkv_one, "fsdp", axis=0, tiled=True))
    proj = proj.astype(jnp.bfloat16)
    query = proj[:, :width]
    key_value = proj[:, width:]
    earlier = [from_behind(key_value, "tm", step) for step in range(LEFT_MAX, 0, -1)]
    gathered = jnp.concatenate(earlier + [key_value], axis=0)
    rows = jnp.arange(fr, dtype=jnp.int32)
    cols = jnp.arange((LEFT_MAX + 1) * fr, dtype=jnp.int32)
    tpos = block * fr + rows[:, None]
    spos = (block - LEFT_MAX) * fr + cols[None, :]
    apart = LEFT_MAX - cols[None, :] // fr
    allowed = (spos >= 0) & (spos <= tpos) & (apart <= count) & ((spos < length) | (spos == tpos))
    ctx_one = attend(query, gathered[:, :width], gathered[:, width:], allowed, HEADS)
    out_proj = add_rows(ctx_one, lax.all_gather(out_one, "fsdp", axis=0, tiled=True))
    hidden = (local.astype(jnp.float32) + out_proj).astype(jnp.bfloat16)
    norm_two = norm_rows(hidden, gain_two)
    proj2 = add_rows(norm_two, lax.all_gather(qkv_two, "fsdp", axis=0, tiled=True))
    proj2 = proj2.astype(jnp.bfloat16)
    query2 = proj2[:, :width]
    key_value2 = proj2[:, width:]
    ahead = from_behind(key_value2[:RIGHT], "tm", -1)
    joined = jnp.concatenate([key_value2, ahead], axis=0)
    cols2 = jnp.arange(fr + RIGHT, dtype=jnp.int32)
    spos2 = block * fr + cols2[None, :]
    allowed2 = (cols2[None, :] <= rows[:, None] + RIGHT) & ((spos2 < length) | (spos2 == tpos))
    ctx_two = attend(query2, joined[:, :width], joined[:, width:], allowed2, HEADS)
    valid = block * fr + rows < length
    context = jnp.where(valid[:, None], ctx_two, jnp.zeros_like(ctx_two))
    weight_grad = lax.psum_scatter(
        lax.dot_general(
            grad_in, context, (((0,), (0,)), ((), ())), preferred_element_type=jnp.float32
        ),
        ("tm", "fsdp"),
        scatter_dimension=0,
        tiled=True,
    )
    return (context[None], weight_grad)


MESH = pl.DeviceIdType.MESH


def flip(index, mask):
    out, bit = index, 1
    while bit <= mask:
        if mask & bit:
            out = out + bit * (1 - 2 * ((index // bit) % 2))
        bit *= 2
    return out


def heads_kernel(
    n,
    nz,
    frames_ref, gain_one_ref, qkv_one_ref, out_one_ref, gain_two_ref, qkv_two_ref,
    length_ref, count_ref, cot_ref,
    context_ref, grad_ref,
    fbuf, nbuf, nbuf2, w1, w2, wo, cotv, cott, gains,
    q1, k1a, k1b, v1a, v1b, p1, r1, ctx1s, ctxall,
    q2, k2a, k2b, v2a, v2b, p2, pn2, r2, ctx2s, ctx2,
    gsend, grecv,
    local_sem, ag_send, ag_recv, ch_recv, cx_recv, nx_recv, one_sem, far_sem,
):
    t = lax.axis_index("tm")
    z = lax.axis_index("fsdp")
    fr, width = frames_ref.shape
    cols = width // n
    head = width // HEADS
    per = HEADS // n
    rows = width // nz
    part = rows // n
    groups = n // 2
    scale = math.log2(math.e) / head**0.5
    mine = pl.multiple_of(t * cols, cols)
    core = lax.rem(t, 2)

    def at_cols(index):
        return pl.ds(pl.multiple_of(index * cols, cols), cols)

    def at_rows(index, size):
        return pl.ds(pl.multiple_of(index * size, size), size)

    barrier = pltpu.get_barrier_semaphore()
    for mask in (4, 2, 1):
        pl.semaphore_signal(barrier, inc=1, device_id=(flip(t, mask), z), device_id_type=MESH)

    @pl.when(z > 0)
    def _():
        pl.semaphore_signal(barrier, inc=1, device_id=(t, z - 1), device_id_type=MESH)

    @pl.when(z < nz - 1)
    def _():
        pl.semaphore_signal(barrier, inc=1, device_id=(t, z + 1), device_id_type=MESH)

    own_rows = at_rows(z, rows)

    def load(src, dst, index):
        return pltpu.make_async_copy(src, dst, local_sem.at[index])

    def load_cols(src, dst, j, index):
        return load(
            src.at[:, pl.ds(pl.multiple_of(j * width + mine, cols), cols)],
            dst.at[own_rows, pl.ds(j * cols, cols)],
            index,
        )

    get_frames = load(frames_ref, fbuf.at[t], 0)
    get_wo = load(out_one_ref, wo.at[pl.ds(0, rows), :], 1)
    get_w1 = [load_cols(qkv_one_ref, w1, j, 2 + j // 2) for j in range(3)]
    get_w2 = [load_cols(qkv_two_ref, w2, j, 4) for j in range(3)]
    get_cot = load(cot_ref, cotv, 5)
    get_gains = [load(gain_one_ref, gains.at[0:1], 6), load(gain_two_ref, gains.at[1:2], 6)]
    for copy in [get_frames, get_wo, *get_w1, *get_gains, get_cot, *get_w2]:
        copy.start()

    def loaded(view, index):
        load(view, view, index).wait()

    CHAIN, CROSS, PAIR, BACK, GRAD, BACK_IN, GRAD_IN = (one_sem.at[i] for i in range(7))

    def sent(sem, view):
        pltpu.make_async_remote_copy(
            src_ref=view, dst_ref=view, send_sem=sem, recv_sem=sem,
            device_id=(flip(t, 1), z), device_id_type=MESH,
        ).wait_send()

    def received(sem, view):
        pltpu.make_async_remote_copy(
            src_ref=view, dst_ref=view, send_sem=sem, recv_sem=sem,
            device_id=(flip(t, 1), z), device_id_type=MESH,
        ).wait_recv()

    half = rows // 2

    NEAR, NEXT, FAR = 0, 1, 2

    def chain_view(which, shard, h, at):
        place = lax.rem(shard - at + nz, nz) if which == 0 else shard
        if h is None:
            span = at_rows(place, rows)
        else:
            span = pl.ds(pl.multiple_of(place * rows + h * half, half), half)
        if which == 0:
            return wo.at[span, pl.ds(mine, cols)]
        wide = pl.ds(0, 2 * cols) if which in (1, 3) else pl.ds(2 * cols, cols)
        return (w1 if which < 3 else w2).at[span, wide]

    def chain_sem(which, shard, h, at):
        apart = lax.rem(shard - at + nz, nz) - 1
        if h is None:
            return ch_recv.at[6 * (nz - 1) + (which - 3) * (nz - 1) + apart]
        return ch_recv.at[(2 * which + h) * (nz - 1) + apart]

    def pieces(which):
        return (0, 1) if which < 3 else (None,)

    def chain_cond(kind, up):
        if kind == NEAR:
            return z < nz - 1 if up else z > 0
        if kind == NEXT:
            return (z > 0) & (z < nz - 1)
        return z == 0 if up else z == nz - 1

    def chain_wait(which, shard, h):
        received(chain_sem(which, shard, h, z), chain_view(which, shard, h, z))

    def chain(which, kind, halves=None):
        for h in halves or pieces(which):
            for up in (True, False):
                @pl.when(chain_cond(kind, up))
                def _():
                    way = 1 if up else -1
                    shard = z - way if kind == NEXT else z
                    to = (nz - 1 if up else 0) if kind == FAR else z + way
                    shard, to = jnp.clip(shard, 0, nz - 1), jnp.clip(to, 0, nz - 1)
                    if kind == NEXT:
                        chain_wait(which, shard, h)
                    pltpu.make_async_remote_copy(
                        src_ref=chain_view(which, shard, h, z),
                        dst_ref=chain_view(which, shard, h, to),
                        send_sem=CHAIN,
                        recv_sem=chain_sem(which, shard, h, to),
                        device_id=(t, to),
                        device_id_type=MESH,
                    ).start()

    def chain_end(which):
        for apart in range(1, nz):
            for way in (1, -1):
                ends = (z == nz - 1) if way == 1 else (z == 0)
                there = z - way * apart
                inside = (there >= 0) & (there < nz)
                @pl.when(inside & ends if apart == 1 else inside)
                def _():
                    for h in pieces(which):
                        chain_wait(which, jnp.clip(there, 0, nz - 1), h)

    def ag_view(which, index, piece):
        if which == 0:
            if piece is None:
                return fbuf.at[index]
            return fbuf.at[index, pl.ds(piece * (fr // 2), fr // 2), :]
        buf, first, size = (
            None, (cott, 0, width // 2), (wo, rows, width - rows), (cott, width // 2, width // 2),
        )[which]
        if piece is None:
            return buf.at[pl.ds(first, size), at_cols(index)]
        return buf.at[pl.ds(first + piece * (size // 2), size // 2), at_cols(index)]

    slots = (
        (0, None, 1), (0, 0, 2), (0, 1, 2), (0, 1, 4), (0, 0, 4),
        (2, 0, 4), (4, 1, 2),
        (2, None, 1), (4, None, 1), (6, 0, 1), (6, 1, 1),
    )

    shared = {1: 0, 3: 1, 2: 2, 4: 3, 5: 4, 6: 5, 0: 6}

    def ag_sem(which, slot):
        if which == 0:
            return ag_recv.at[shared.get(slot, 7 if slot < 9 else 8)]
        return ag_recv.at[9 + 7 * (which - 1) + shared.get(slot, 6)]

    def ag_copy(which, slot):
        block, piece, to = slots[slot]
        view = ag_view(which, flip(t, block), piece)
        return pltpu.make_async_remote_copy(
            src_ref=view, dst_ref=view,
            send_sem=ag_send.at[which], recv_sem=ag_sem(which, slot),
            device_id=(flip(t, to), z), device_id_type=MESH,
        )

    def ag_wait(which, slot):
        block, piece, to = slots[slot]
        received(ag_sem(which, slot), ag_view(which, flip(t, block ^ to), piece))

    def ag_start(which):
        for slot in (1, 3, 2, 4, 0):
            ag_copy(which, slot).start()

    def ag_forward(which, stage):
        for waits, slot in (
            (((1, 5), (3, 6)), ((2, 7), (4, 8)), ((5, 9), (6, 10)))[stage]
        ):
            ag_wait(which, waits)
            ag_copy(which, slot).start()

    def ag_many(which, blocks):
        if which == 0:
            return fbuf.at[0:blocks]
        first = (0, 0, rows, 0)[which]
        size = width - rows if which == 2 else width // 2
        return (wo if which == 2 else cott).at[first : first + size, 0 : blocks * cols]

    def ag_partner(which):
        received(ag_sem(which, 0), ag_many(which, 4))

    def ag_sent(which):
        sent(ag_send.at[which], ag_many(which, n - 1))

    def normed(index):
        nbuf[index] = norm_rows(fbuf[index], gains[0:1, :])

    def masked_heads(values):
        lane = lax.broadcasted_iota(jnp.int32, values.shape, 1) // head
        blank = jnp.zeros_like(values)
        return jnp.where(lane == 0, values, blank), jnp.where(lane == 1, values, blank)

    def dot(left, right):
        return jnp.dot(left, right, preferred_element_type=jnp.float32)

    def dot_t(left, right):
        return lax.dot_general(
            left, right, (((1,), (1,)), ((), ())), preferred_element_type=jnp.float32
        )

    def project(buf, weight, pair, targets_qk, targets_v):
        left = buf[2 * pair : 2 * pair + 2].reshape(2 * fr, width)
        span = pl.ds(2 * pair * fr, 2 * fr)
        if targets_qk is not None:
            q, ka, kb = targets_qk
            out = dot(left, weight[:, : 2 * cols]).astype(jnp.bfloat16)
            q[span, :] = out[:, :cols]
            ka[span, :], kb[span, :] = masked_heads(out[:, cols:])
        else:
            va, vb = targets_v
            out = dot(left, weight[:, 2 * cols :]).astype(jnp.bfloat16)
            va[span, :], vb[span, :] = masked_heads(out)

    def turned(index):
        return lax.rem(index - z * (rows // cols) + n, n)

    with mark("a_barrier"):
        pl.semaphore_wait(
            barrier, 3 + jnp.where(z > 0, 1, 0) + jnp.where(z < nz - 1, 1, 0)
        )
    with mark("b_frames"):
        get_frames.wait()
    ag_start(0)
    get_wo.wait()
    chain(0, NEAR)
    inner = (z > 0) & (z < nz - 1)
    lower = z < nz // 2

    @pl.when(inner)
    def _():
        other = jnp.clip(jnp.where(lower, z + 1, z - 1), 0, nz - 1)
        pl.semaphore_signal(far_sem, inc=1, device_id=(t, other), device_id_type=MESH)

    loaded(w1.at[own_rows, 0 : 2 * cols], 2)
    chain(1, NEAR, (0,))
    with mark("d_norm"):
        loaded(gains, 6)
        normed(t)
    with mark("e_far"):
        @pl.when(inner)
        def _():
            edge = jnp.clip(jnp.where(lower, z - 1, z + 1), 0, nz - 1)
            pl.semaphore_wait(far_sem, 1)
            pl.semaphore_signal(far_sem, inc=1, device_id=(t, edge), device_id_type=MESH)

    with mark("e_next0"):
        chain(0, NEXT)
    chain(1, NEAR, (1,))
    with mark("e_edge"):
        @pl.when((z == 0) | (z == nz - 1))
        def _():
            pl.semaphore_wait(far_sem, 1)

    chain(0, FAR)
    chain(1, FAR)
    with mark("f_agf00"):
        ag_forward(0, 0)
    with mark("g_turn"):
        get_cot.wait()
        turned_cot = cotv[...].T
        for zz in range(nz):
            for tt in range(n):
                cott[zz * rows + tt * part : zz * rows + (tt + 1) * part, pl.ds(mine, cols)] = (
                    turned_cot[(tt * nz + zz) * part : (tt * nz + zz + 1) * part]
                )
        ag_wait(0, 0)
        normed(flip(t, 1))
    with mark("i_agf01"):
        ag_forward(0, 1)
    with mark("j_next1a"):
        chain(1, NEXT, (0,))
    with mark("k_chainend0"):
        chain_end(0)
    ag_start(2)
    with mark("l_norms"):
        normed(flip(t, 2))
        normed(flip(t, 4))
    with mark("m_next1b"):
        chain(1, NEXT, (1,))
    loaded(w1.at[own_rows, 2 * cols : 3 * cols], 3)
    chain(2, NEAR)
    chain(2, FAR)
    with mark("n_agf02"):
        ag_forward(0, 2)
    with mark("o_norms"):
        received(ag_sem(0, 7), ag_many(0, 2))
        normed(flip(t, 3))
        normed(flip(t, 5))
        normed(flip(t, 6))
    with mark("q_agf20"):
        ag_forward(2, 0)
    ag_start(1)
    with mark("p_norm"):
        received(ag_sem(0, 9), ag_many(0, 1))
        normed(flip(t, 7))
    with mark("r_chainend1"):
        chain_end(1)
    with mark("ra_next2"):
        chain(2, NEXT)
    with mark("s_projqk"):
        for pair in range(groups):
            project(nbuf, w1, pair, (q1, k1a, k1b), None)

    length = length_ref[0]
    count = count_ref[0]
    row = lax.broadcasted_iota(jnp.int32, (fr, fr), 0)
    col = lax.broadcasted_iota(jnp.int32, (fr, fr), 1)
    low = -1e30

    def spans(b):
        first = max(b - LEFT_MAX, 0)
        return pl.ds(first * fr, (b + 1 - first) * fr), b - first

    def causal(b):
        span, before = spans(b)
        size = (before + 1) * fr
        query = q1[b * fr : (b + 1) * fr, :]
        both = dot_t(query, jnp.concatenate([k1a[span, :], k1b[span, :]], axis=0))
        spos = (b - before) * fr + lax.broadcasted_iota(jnp.int32, (1, size), 1)
        apart = before - lax.broadcasted_iota(jnp.int32, (1, size), 1) // fr
        bias = jnp.where((apart <= count) & (spos < length), 0.0, low)
        expos, inverse = [], []
        for h in range(per):
            scores = both[:, h * size : (h + 1) * size]
            now = scores[:, before * fr :]
            now = jnp.where(
                row > col,
                now + bias[:, before * fr :],
                jnp.where(row == col, now, low),
            )
            if before:
                now = jnp.concatenate(
                    [scores[:, : before * fr] + bias[:, : before * fr], now], axis=1
                )
            top = jnp.max(now, axis=-1, keepdims=True)
            expo = jnp.exp2((now - top) * scale)
            inverse.append(1.0 / jnp.sum(expo, axis=-1, keepdims=True))
            expos.append(expo.astype(jnp.bfloat16))
        p1[b, :, : per * size] = jnp.concatenate(expos, axis=1)
        r1[b] = jnp.where(col // head == 0, inverse[0], inverse[1])

    def causal_mix(b):
        span, before = spans(b)
        size = (before + 1) * fr
        mixed = dot(
            p1[b, :, : per * size], jnp.concatenate([v1a[span, :], v1b[span, :]], axis=0)
        )
        ctx1s[b * fr : (b + 1) * fr, :] = (mixed * r1[b]).astype(jnp.bfloat16)

    with mark("t_soft0"):
        causal(0)
        causal(1)
    with mark("ta_agf21"):
        ag_forward(2, 1)
    with mark("t_soft1"):
        causal(2)
        causal(3)
    with mark("td_agf22"):
        ag_forward(2, 2)
    with mark("t_soft2"):
        causal(4)
        causal(5)
        causal(6)
        causal(7)
    with mark("u_agf10"):
        ag_forward(1, 0)
    loaded(w2.at[own_rows, :], 4)
    chain(3, NEAR)
    with mark("v_chainend2"):
        chain_end(2)
    chain(3, FAR)
    with mark("w_projv"):
        for pair in range(groups):
            project(nbuf, w1, pair, None, (v1a, v1b))

    def cx_copy(g, m):
        to = flip(t, (m, 4, 2)[max(m - 5, 0)])
        if m < 6:
            src = ctx1s.at[at_rows(2 * g + lax.rem(core + m, 2), fr), :]
            dst = ctxall.at[g, :, at_cols(turned(t))]
        else:
            first = turned(flip(t, 2 if m == 6 else 4) // 2 * 2)
            src = ctxall.at[
                g,
                pl.ds((m - 6) * (fr // 2), fr // 2),
                pl.ds(pl.multiple_of(first * cols, 2 * cols), 2 * cols),
            ]
            dst = src
        return pltpu.make_async_remote_copy(
            src_ref=src, dst_ref=dst,
            send_sem=CROSS, recv_sem=cx_recv.at[3 * g + (0, 2, 0, 0, 1, 1, 2, 2)[m]],
            device_id=(to, z), device_id_type=MESH,
        )

    def cx_wait(g, kind):
        received(cx_recv.at[3 * g + kind], ctxall.at[g, :, 0 : (2, 2, 3)[kind] * cols])

    def cx_forward(g):
        cx_wait(g, 0)
        cx_copy(g, 6).start()
        cx_wait(g, 1)
        cx_copy(g, 7).start()

    def cx_send(g):
        for m in (2, 4, 3, 5, 1):
            cx_copy(g, m).start()

    with mark("x_mix"):
        for g in range(groups):
            causal_mix(2 * g)
            causal_mix(2 * g + 1)
            if g < 3:
                cx_send(g)
            ctxall[g, :, at_cols(turned(t))] = ctx1s[at_rows(2 * g + core, fr), :]
    chain(4, NEAR)
    with mark("xa_agf11"):
        ag_forward(1, 1)
    with mark("xb_next3"):
        chain(3, NEXT)
    chain(4, FAR)
    with mark("xd_fwd0"):
        cx_forward(0)
    cx_send(3)
    with mark("xc_agf12"):
        ag_forward(1, 2)
    with mark("xe_fwd1"):
        cx_forward(1)
    with mark("xf_agp2"):
        ag_partner(2)

    def nx_copy(g, other):
        view = nbuf2.at[2 * g + (1 - core if other else core)]
        return pltpu.make_async_remote_copy(
            src_ref=view, dst_ref=view,
            send_sem=PAIR, recv_sem=nx_recv.at[g],
            device_id=(flip(t, 1), z), device_id_type=MESH,
        )

    def out_block(g):
        cx_wait(g, 2)
        b = 2 * g + core
        mixed = dot(ctxall[g], wo[...])
        hidden = (fbuf[b].astype(jnp.float32) + mixed).astype(jnp.bfloat16)
        nbuf2[b] = norm_rows(hidden, gains[1:2, :])
        nx_copy(g, False).start()

    tail = -(-RIGHT // 16) * 16
    wide = lax.broadcasted_iota(jnp.int32, (tail, tail), 1)
    long = lax.broadcasted_iota(jnp.int32, (tail, tail), 0) + (fr - tail)

    def ahead(b):
        query = q2[b * fr : (b + 1) * fr, :]
        here = pl.ds(b * fr, fr)
        both = dot_t(query, jnp.concatenate([k2a[here, :], k2b[here, :]], axis=0))
        seen = jnp.where(b * fr + lax.broadcasted_iota(jnp.int32, (1, fr), 1) < length, 0.0, low)
        after = None
        if b < n - 1:
            there = pl.ds((b + 1) * fr, tail)
            after = dot_t(
                query[fr - tail :], jnp.concatenate([k2a[there, :], k2b[there, :]], axis=0)
            )
            spos = (b + 1) * fr + lax.broadcasted_iota(jnp.int32, (1, tail), 1)
            late = jnp.where(spos < length, 0.0, low)
        expos, lates, inverse = [], [], []
        for h in range(per):
            now = both[:, h * fr : (h + 1) * fr]
            now = jnp.where(
                row == col, now, jnp.where(col <= row + RIGHT, now + seen, low)
            )
            top = jnp.max(now, axis=-1, keepdims=True)
            if after is not None:
                then = after[:, h * tail : (h + 1) * tail]
                then = jnp.where(wide + fr <= long + RIGHT, then + late, low)
                top = jnp.concatenate(
                    [
                        top[: fr - tail],
                        jnp.maximum(top[fr - tail :], jnp.max(then, axis=-1, keepdims=True)),
                    ],
                    axis=0,
                )
            expo = jnp.exp2((now - top) * scale)
            total = jnp.sum(expo, axis=-1, keepdims=True)
            if after is not None:
                then = jnp.exp2((then - top[fr - tail :]) * scale)
                total = jnp.concatenate(
                    [
                        total[: fr - tail],
                        total[fr - tail :] + jnp.sum(then, axis=-1, keepdims=True),
                    ],
                    axis=0,
                )
                lates.append(then.astype(jnp.bfloat16))
            inverse.append(1.0 / total)
            expos.append(expo.astype(jnp.bfloat16))
        p2[b] = jnp.concatenate(expos, axis=1)
        if after is not None:
            pn2[b] = jnp.concatenate(lates, axis=1)
        valid = b * fr + row < length
        r2[b] = jnp.where(valid, jnp.where(col // head == 0, inverse[0], inverse[1]), 0.0)

    def ahead_mix(b):
        here = pl.ds(b * fr, fr)
        mixed = dot(p2[b], jnp.concatenate([v2a[here, :], v2b[here, :]], axis=0))
        if b < n - 1:
            there = pl.ds((b + 1) * fr, tail)
            extra = dot(pn2[b], jnp.concatenate([v2a[there, :], v2b[there, :]], axis=0))
            mixed = jnp.concatenate([mixed[: fr - tail], mixed[fr - tail :] + extra], axis=0)
        ctx2s[b * fr : (b + 1) * fr, :] = (mixed * r2[b]).astype(jnp.bfloat16)

    def second(g):
        nx_copy(g, True).wait_recv()
        project(nbuf2, w2, g, (q2, k2a, k2b), None)
        if g:
            ahead(2 * g - 1)
        ahead(2 * g)

    with mark("y_out0"):
        out_block(0)
    with mark("ya_fwd2"):
        cx_forward(2)
    with mark("yb_next4"):
        chain(4, NEXT)
    with mark("y_out1"):
        out_block(1)
    with mark("yc_fwd3"):
        cx_forward(3)
    ag_start(3)
    with mark("yd_chainend3"):
        chain_end(3)
    with mark("ye_second0"):
        second(0)
    with mark("y_out2"):
        out_block(2)
    with mark("ye_second1"):
        second(1)
    with mark("yg_agf30"):
        ag_forward(3, 0)
    with mark("y_out3"):
        out_block(3)
    with mark("yh_agf31"):
        ag_forward(3, 1)
    with mark("ye_second2"):
        second(2)
    with mark("yk_agf32"):
        ag_forward(3, 2)
    with mark("yf_agp1"):
        ag_partner(1)
    with mark("ye_second3"):
        second(3)
        ahead(n - 1)
    with mark("yi_chainend4"):
        chain_end(4)
    with mark("yj_mix2"):
        for g in range(groups):
            project(nbuf2, w2, g, None, (v2a, v2b))
        for b in range(n):
            ahead_mix(b)
    with mark("yl_agp3"):
        ag_partner(3)

    def back_copy(d):
        return pltpu.make_async_remote_copy(
            src_ref=ctx2s.at[at_rows(lax.rem(t + d, n), fr), :],
            dst_ref=ctx2.at[:, at_cols(t)],
            send_sem=BACK, recv_sem=BACK_IN,
            device_id=(lax.rem(t + d, n), z), device_id_type=MESH,
        )

    def grad_copy(m, d):
        to = lax.rem(t + d, n)
        return pltpu.make_async_remote_copy(
            src_ref=gsend.at[m, at_rows(to, part), :],
            dst_ref=grecv.at[m, :, at_cols(t)],
            send_sem=GRAD, recv_sem=GRAD_IN,
            device_id=(to, flip(z, m) if m else z), device_id_type=MESH,
        )

    with mark("z_terms"):
        for m in (3, 2, 1, 0):
            zz = flip(z, m) if m else z
            gsend[m] = dot(cott[at_rows(zz, rows), :], ctx2s[...]).astype(jnp.bfloat16)
            for d in range(1 if m == 0 else 0, n):
                grad_copy(m, d).start()
        grecv[0, :, at_cols(t)] = gsend[0, at_rows(t, part), :]
        for d in range(1, n):
            back_copy(d).start()
        ctx2[:, at_cols(t)] = ctx2s[at_rows(t, fr), :]
    with mark("za_grads"):
        received(GRAD_IN, ctx2s.at[0 : (n * nz - 1) * part, :])
        total = grecv[0].astype(jnp.float32)
        for m in range(1, nz):
            total = total + grecv[m].astype(jnp.float32)
        grad_ref[...] = total
    with mark("zb_back"):
        received(BACK_IN, ctx2.at[:, 0 : (n - 1) * cols])
        context_ref[...] = ctx2[...]
    with mark("zd_sent"):
        for which in range(4):
            ag_sent(which)
        whole = 7 * rows * cols // width

        @pl.when((z == 0) | (z == nz - 1))
        def _():
            sent(CHAIN, cott.at[0 : 2 * whole, :])

        @pl.when((z > 0) & (z < nz - 1))
        def _():
            sent(CHAIN, cott.at[0 : 4 * whole, :])

        sent(CROSS, cott.at[0 : 7 * groups * fr * cols // width, :])
        sent(PAIR, nbuf2.at[0:groups])
        sent(BACK, ctx2.at[:, 0 : (n - 1) * cols])
        sent(GRAD, ctx2s.at[0 : (n * nz - 1) * part, :])


def hand_out(context_ref, grad_ref, context_out, grad_out):
    context_out[...] = context_ref[...]
    grad_out[...] = grad_ref[...]


def by_heads(
    n, nz, frames, gain_one, qkv_one, out_one, gain_two, qkv_two, lengths, left_counts, cotangent
):
    _, fr, width = frames.shape
    cols = width // n
    rows = width // nz
    span = n * fr
    tail = -(-RIGHT // 16) * 16
    per = HEADS // n
    vmem = pl.BlockSpec(memory_space=pltpu.VMEM)
    smem = pl.BlockSpec(memory_space=pltpu.SMEM)
    hbm = pl.BlockSpec(memory_space=pltpu.HBM)
    bf16, f32 = jnp.bfloat16, jnp.float32
    dma = pltpu.SemaphoreType.DMA
    large = (
        frames[0], gain_one[None], qkv_one, out_one, gain_two[None], qkv_two, cotangent[0],
    )
    large = [pltpu.with_memory_space_constraint(value, pltpu.HBM) for value in large]
    context, grad = pl.pallas_call(
        functools.partial(heads_kernel, n, nz),
        out_shape=(
            jax.ShapeDtypeStruct((fr, width), bf16),
            jax.ShapeDtypeStruct((rows // n, width), f32),
        ),
        in_specs=[hbm] * 6 + [smem] * 2 + [hbm],
        out_specs=(vmem, vmem),
        scratch_shapes=[
            pltpu.VMEM((n, fr, width), bf16),
            pltpu.VMEM((n, fr, width), bf16),
            pltpu.VMEM((n, fr, width), bf16),
            pltpu.VMEM((width, 3 * cols), bf16),
            pltpu.VMEM((width, 3 * cols), bf16),
            pltpu.VMEM((width, width), bf16),
            pltpu.VMEM((fr, width), bf16),
            pltpu.VMEM((width, span), bf16),
            pltpu.VMEM((2, width), f32),
            *[pltpu.VMEM((span, cols), bf16)] * 5,
            pltpu.VMEM((n, fr, per * (LEFT_MAX + 1) * fr), bf16),
            pltpu.VMEM((n, fr, cols), f32),
            pltpu.VMEM((span, cols), bf16),
            pltpu.VMEM((n // 2, fr, width), bf16),
            *[pltpu.VMEM((span, cols), bf16)] * 5,
            pltpu.VMEM((n, fr, per * fr), bf16),
            pltpu.VMEM((n, tail, per * tail), bf16),
            pltpu.VMEM((n, fr, cols), f32),
            pltpu.VMEM((span, cols), bf16),
            pltpu.VMEM((fr, width), bf16),
            pltpu.VMEM((nz, rows, cols), bf16),
            pltpu.VMEM((nz, rows // n, width), bf16),
            dma((7,)),
            dma((4,)),
            dma((30,)),
            dma((8 * (nz - 1),)),
            dma((3 * n // 2,)),
            dma((n // 2,)),
            dma((7,)),
            pltpu.SemaphoreType.REGULAR,
        ],
        compiler_params=pltpu.CompilerParams(
            collective_id=0, has_side_effects=True, vmem_limit_bytes=44 * 1024 * 1024
        ),
    )(*large[:6], lengths, left_counts, large[6])
    context, grad = pl.pallas_call(
        hand_out,
        out_shape=(
            jax.ShapeDtypeStruct((fr, width), bf16),
            jax.ShapeDtypeStruct((rows // n, width), f32),
        ),
        in_specs=[vmem, vmem],
        out_specs=(vmem, vmem),
        compiler_params=pltpu.CompilerParams(vmem_limit_bytes=4 * 1024 * 1024),
    )(context, grad)
    return (context[None], grad)


def solution(mesh):
    n_tm = mesh.shape["tm"]
    even = n_tm == 2 * CHIPS and mesh.shape["fsdp"] == CHIPS and HEADS == 2 * n_tm
    chosen = functools.partial(by_heads, n_tm, mesh.shape["fsdp"]) if even else on_device
    in_specs = (
        P("fsdp", "tm", None),
        P(),
        P("fsdp", None),
        P("fsdp", None),
        P(),
        P("fsdp", None),
        P("fsdp"),
        P("fsdp"),
        P("fsdp", "tm", None),
    )
    out_specs = (P("fsdp", "tm", None), P(("tm", "fsdp"), None))
    return jax.shard_map(
        chosen, mesh=mesh, in_specs=in_specs, out_specs=out_specs, check_vma=False
    )
```

```python
import contextlib
import functools
import math

import jax
import jax.numpy as jnp
from jax import lax
from jax.experimental import pallas as pl
from jax.experimental.pallas import tpu as pltpu
from jax.sharding import PartitionSpec as P

HEADS = 16
LEFT_MAX = 2
RIGHT = 23
CHIPS = 4
SCOPES = False


def mark(name):
    return jax.named_scope(name) if SCOPES else contextlib.nullcontext()


def from_behind(block, axis, distance):
    devices = range(lax.axis_size(axis))
    route = [(i - distance, i) for i in devices if i - distance in devices]
    return lax.ppermute(block, axis, route)


def norm_rows(values, gain):
    wide = values.astype(jnp.float32)
    mean = jnp.mean(wide, axis=-1, keepdims=True)
    var = jnp.mean((wide - mean) ** 2, axis=-1, keepdims=True)
    return ((wide - mean) * lax.rsqrt(var + 1e-05) * gain).astype(jnp.bfloat16)


def attend(query, keys, values, allowed, heads):
    rows_q, width = query.shape
    head = width // heads
    scale = 1.0 / head**0.5
    q_heads = query.reshape(rows_q, heads, head)
    k_heads = keys.reshape(keys.shape[0], heads, head)
    v_heads = values.reshape(values.shape[0], heads, head)
    scores = (
        jnp.einsum("qhe,khe->hqk", q_heads, k_heads, preferred_element_type=jnp.float32) * scale
    )
    scores = jnp.where(allowed[None], scores, -1e30)
    top = jnp.max(scores, axis=-1, keepdims=True)
    expo = jnp.exp(scores - top)
    weights = (expo / jnp.sum(expo, axis=-1, keepdims=True)).astype(jnp.bfloat16)
    ctx = jnp.einsum("hqk,khe->qhe", weights, v_heads, preferred_element_type=jnp.float32)
    return ctx.reshape(rows_q, width).astype(jnp.bfloat16)


def add_rows(left, piece):
    return jnp.dot(left, piece, preferred_element_type=jnp.float32)


def on_device(
    frames, gain_one, qkv_one, out_one, gain_two, qkv_two, lengths, left_counts, cotangent
):
    local = frames[0]
    grad_in = cotangent[0]
    fr, width = local.shape
    block = lax.axis_index("tm")
    length = lengths[0]
    count = left_counts[0]
    norm_one = norm_rows(local, gain_one)
    proj = add_rows(norm_one, lax.all_gather(qkv_one, "fsdp", axis=0, tiled=True))
    proj = proj.astype(jnp.bfloat16)
    query = proj[:, :width]
    key_value = proj[:, width:]
    earlier = [from_behind(key_value, "tm", step) for step in range(LEFT_MAX, 0, -1)]
    gathered = jnp.concatenate(earlier + [key_value], axis=0)
    rows = jnp.arange(fr, dtype=jnp.int32)
    cols = jnp.arange((LEFT_MAX + 1) * fr, dtype=jnp.int32)
    tpos = block * fr + rows[:, None]
    spos = (block - LEFT_MAX) * fr + cols[None, :]
    apart = LEFT_MAX - cols[None, :] // fr
    allowed = (spos >= 0) & (spos <= tpos) & (apart <= count) & ((spos < length) | (spos == tpos))
    ctx_one = attend(query, gathered[:, :width], gathered[:, width:], allowed, HEADS)
    out_proj = add_rows(ctx_one, lax.all_gather(out_one, "fsdp", axis=0, tiled=True))
    hidden = (local.astype(jnp.float32) + out_proj).astype(jnp.bfloat16)
    norm_two = norm_rows(hidden, gain_two)
    proj2 = add_rows(norm_two, lax.all_gather(qkv_two, "fsdp", axis=0, tiled=True))
    proj2 = proj2.astype(jnp.bfloat16)
    query2 = proj2[:, :width]
    key_value2 = proj2[:, width:]
    ahead = from_behind(key_value2[:RIGHT], "tm", -1)
    joined = jnp.concatenate([key_value2, ahead], axis=0)
    cols2 = jnp.arange(fr + RIGHT, dtype=jnp.int32)
    spos2 = block * fr + cols2[None, :]
    allowed2 = (cols2[None, :] <= rows[:, None] + RIGHT) & ((spos2 < length) | (spos2 == tpos))
    ctx_two = attend(query2, joined[:, :width], joined[:, width:], allowed2, HEADS)
    valid = block * fr + rows < length
    context = jnp.where(valid[:, None], ctx_two, jnp.zeros_like(ctx_two))
    weight_grad = lax.psum_scatter(
        lax.dot_general(
            grad_in, context, (((0,), (0,)), ((), ())), preferred_element_type=jnp.float32
        ),
        ("tm", "fsdp"),
        scatter_dimension=0,
        tiled=True,
    )
    return (context[None], weight_grad)


MESH = pl.DeviceIdType.MESH


def flip(index, mask):
    out, bit = index, 1
    while bit <= mask:
        if mask & bit:
            out = out + bit * (1 - 2 * ((index // bit) % 2))
        bit *= 2
    return out


def heads_kernel(
    n,
    nz,
    frames_ref, gain_one_ref, qkv_one_ref, out_one_ref, gain_two_ref, qkv_two_ref,
    length_ref, count_ref, cot_ref,
    context_ref, grad_ref,
    fbuf, nbuf, nbuf2, w1, w2, wo, cotv, cott, gains,
    q1, k1a, k1b, v1a, v1b, p1, r1, ctx1s, ctxall,
    q2, k2a, k2b, v2a, v2b, p2, pn2, r2, ctx2s, ctx2,
    gsend, grecv, fsum, pbuf,
    local_sem, ag_send, ag_recv, ch_recv, cx_recv, nx_recv, one_sem, far_sem, pre_sem,
):
    t = lax.axis_index("tm")
    z = lax.axis_index("fsdp")
    fr, width = frames_ref.shape
    cols = width // n
    head = width // HEADS
    per = HEADS // n
    rows = width // nz
    part = rows // n
    groups = n // 2
    scale = math.log2(math.e) / head**0.5
    mine = pl.multiple_of(t * cols, cols)
    core = lax.rem(t, 2)

    def at_cols(index):
        return pl.ds(pl.multiple_of(index * cols, cols), cols)

    def at_rows(index, size):
        return pl.ds(pl.multiple_of(index * size, size), size)

    barrier = pltpu.get_barrier_semaphore()
    for mask in (4, 2, 1):
        pl.semaphore_signal(barrier, inc=1, device_id=(flip(t, mask), z), device_id_type=MESH)

    @pl.when(z > 0)
    def _():
        pl.semaphore_signal(barrier, inc=1, device_id=(t, z - 1), device_id_type=MESH)

    @pl.when(z < nz - 1)
    def _():
        pl.semaphore_signal(barrier, inc=1, device_id=(t, z + 1), device_id_type=MESH)

    own_rows = at_rows(z, rows)

    def load(src, dst, index):
        return pltpu.make_async_copy(src, dst, local_sem.at[index])

    def load_cols(src, dst, j, index):
        return load(
            src.at[:, pl.ds(pl.multiple_of(j * width + mine, cols), cols)],
            dst.at[own_rows, pl.ds(j * cols, cols)],
            index,
        )

    get_frames = load(frames_ref, fbuf.at[t], 0)
    get_wo = load(out_one_ref, wo.at[pl.ds(0, rows), :], 1)
    get_w1 = [load_cols(qkv_one_ref, w1, j, 2 + j // 2) for j in range(3)]
    get_w2 = [load_cols(qkv_two_ref, w2, j, 4) for j in range(3)]
    get_cot = load(cot_ref, cotv, 5)
    get_gains = [load(gain_one_ref, gains.at[0:1], 6), load(gain_two_ref, gains.at[1:2], 6)]
    for copy in [get_frames, get_wo, *get_w1, *get_gains, get_cot, *get_w2]:
        copy.start()

    def loaded(view, index):
        load(view, view, index).wait()

    CHAIN, CROSS, PAIR, BACK, GRAD, BACK_IN, GRAD_IN = (one_sem.at[i] for i in range(7))

    def sent(sem, view):
        pltpu.make_async_remote_copy(
            src_ref=view, dst_ref=view, send_sem=sem, recv_sem=sem,
            device_id=(flip(t, 1), z), device_id_type=MESH,
        ).wait_send()

    def received(sem, view):
        pltpu.make_async_remote_copy(
            src_ref=view, dst_ref=view, send_sem=sem, recv_sem=sem,
            device_id=(flip(t, 1), z), device_id_type=MESH,
        ).wait_recv()

    half = rows // 2

    NEAR, NEXT, FAR = 0, 1, 2

    def chain_view(which, shard, h, at):
        place = lax.rem(shard - at + nz, nz) if which == 0 else shard
        if h is None:
            span = at_rows(place, rows)
        else:
            span = pl.ds(pl.multiple_of(place * rows + h * half, half), half)
        if which == 0:
            return wo.at[span, pl.ds(mine, cols)]
        wide = pl.ds(0, 2 * cols) if which in (1, 3) else pl.ds(2 * cols, cols)
        return (w1 if which < 3 else w2).at[span, wide]

    def chain_sem(which, shard, h, at):
        apart = lax.rem(shard - at + nz, nz) - 1
        if h is None:
            return ch_recv.at[6 * (nz - 1) + (which - 3) * (nz - 1) + apart]
        return ch_recv.at[(2 * which + h) * (nz - 1) + apart]

    def pieces(which):
        return (0, 1) if which < 3 else (None,)

    def chain_cond(kind, up):
        if kind == NEAR:
            return z < nz - 1 if up else z > 0
        if kind == NEXT:
            return (z > 0) & (z < nz - 1)
        return z == 0 if up else z == nz - 1

    def chain_wait(which, shard, h):
        received(chain_sem(which, shard, h, z), chain_view(which, shard, h, z))

    def chain(which, kind, halves=None):
        for h in halves or pieces(which):
            for up in (True, False):
                @pl.when(chain_cond(kind, up))
                def _():
                    way = 1 if up else -1
                    shard = z - way if kind == NEXT else z
                    to = (nz - 1 if up else 0) if kind == FAR else z + way
                    shard, to = jnp.clip(shard, 0, nz - 1), jnp.clip(to, 0, nz - 1)
                    if kind == NEXT:
                        chain_wait(which, shard, h)
                    pltpu.make_async_remote_copy(
                        src_ref=chain_view(which, shard, h, z),
                        dst_ref=chain_view(which, shard, h, to),
                        send_sem=CHAIN,
                        recv_sem=chain_sem(which, shard, h, to),
                        device_id=(t, to),
                        device_id_type=MESH,
                    ).start()

    def chain_end(which):
        for apart in range(1, nz):
            for way in (1, -1):
                ends = (z == nz - 1) if way == 1 else (z == 0)
                there = z - way * apart
                inside = (there >= 0) & (there < nz)
                @pl.when(inside & ends if apart == 1 else inside)
                def _():
                    for h in pieces(which):
                        chain_wait(which, jnp.clip(there, 0, nz - 1), h)

    early = width * 5 // 8

    def ag_view(which, index, piece):
        if which == 0:
            if piece is None:
                return fbuf.at[index]
            return fbuf.at[index, pl.ds(piece * (fr // 2), fr // 2), :]
        buf, first, size = (
            None, (cott, 0, early), (wo, rows, width - rows), (cott, early, width - early),
        )[which]
        if piece is None:
            return buf.at[pl.ds(first, size), at_cols(index)]
        return buf.at[pl.ds(first + piece * (size // 2), size // 2), at_cols(index)]

    slots = (
        (0, None, 1), (0, 0, 2), (0, 1, 2), (0, 1, 4), (0, 0, 4),
        (2, 0, 4), (4, 1, 2),
        (2, None, 1), (4, None, 1), (6, 0, 1), (6, 1, 1),
    )

    shared = {1: 0, 3: 1, 2: 2, 4: 3, 5: 4, 6: 5, 0: 6}

    def ag_sem(which, slot):
        if which == 0:
            return ag_recv.at[shared.get(slot, 7 if slot < 9 else 8)]
        return ag_recv.at[9 + 7 * (which - 1) + shared.get(slot, 6)]

    def ag_copy(which, slot):
        block, piece, to = slots[slot]
        view = ag_view(which, flip(t, block), piece)
        return pltpu.make_async_remote_copy(
            src_ref=view, dst_ref=view,
            send_sem=ag_send.at[which], recv_sem=ag_sem(which, slot),
            device_id=(flip(t, to), z), device_id_type=MESH,
        )

    def ag_wait(which, slot):
        block, piece, to = slots[slot]
        received(ag_sem(which, slot), ag_view(which, flip(t, block ^ to), piece))

    def ag_start(which):
        for slot in (1, 3, 2, 4, 0):
            ag_copy(which, slot).start()

    def ag_forward(which, stage):
        for waits, slot in (
            (((1, 5), (3, 6)), ((2, 7), (4, 8)), ((5, 9), (6, 10)))[stage]
        ):
            ag_wait(which, waits)
            ag_copy(which, slot).start()

    def ag_many(which, blocks):
        if which == 0:
            return fbuf.at[0:blocks]
        first = (0, 0, rows, early)[which]
        size = (0, early, width - rows, width - early)[which]
        return (wo if which == 2 else cott).at[first : first + size, 0 : blocks * cols]

    def ag_partner(which):
        received(ag_sem(which, 0), ag_many(which, 4))

    def ag_sent(which):
        sent(ag_send.at[which], ag_many(which, n - 1))

    def normed(index):
        nbuf[index] = norm_rows(fbuf[index], gains[0:1, :])

    def masked_heads(values):
        lane = lax.broadcasted_iota(jnp.int32, values.shape, 1) // head
        blank = jnp.zeros_like(values)
        return jnp.where(lane == 0, values, blank), jnp.where(lane == 1, values, blank)

    def dot(left, right):
        return jnp.dot(left, right, preferred_element_type=jnp.float32)

    def dot_t(left, right):
        return lax.dot_general(
            left, right, (((1,), (1,)), ((), ())), preferred_element_type=jnp.float32
        )

    def project(buf, weight, pair, targets_qk, targets_v):
        left = buf[2 * pair : 2 * pair + 2].reshape(2 * fr, width)
        span = pl.ds(2 * pair * fr, 2 * fr)
        if targets_qk is not None:
            q, ka, kb = targets_qk
            out = dot(left, weight[:, : 2 * cols]).astype(jnp.bfloat16)
            q[span, :] = out[:, :cols]
            ka[span, :], kb[span, :] = masked_heads(out[:, cols:])
        else:
            va, vb = targets_v
            out = dot(left, weight[:, 2 * cols :]).astype(jnp.bfloat16)
            va[span, :], vb[span, :] = masked_heads(out)

    def turned(index):
        return lax.rem(index - z * (rows // cols) + n, n)

    with mark("a_barrier"):
        pl.semaphore_wait(
            barrier, 3 + jnp.where(z > 0, 1, 0) + jnp.where(z < nz - 1, 1, 0)
        )
    with mark("b_frames"):
        get_frames.wait()
    ag_start(0)
    get_wo.wait()
    chain(0, NEAR)
    inner = (z > 0) & (z < nz - 1)
    lower = z < nz // 2

    @pl.when(inner)
    def _():
        other = jnp.clip(jnp.where(lower, z + 1, z - 1), 0, nz - 1)
        pl.semaphore_signal(far_sem, inc=1, device_id=(t, other), device_id_type=MESH)

    loaded(w1.at[own_rows, 0 : 2 * cols], 2)
    chain(1, NEAR, (0,))
    with mark("d_norm"):
        loaded(gains, 6)
        normed(t)
    with mark("e_far"):
        @pl.when(inner)
        def _():
            edge = jnp.clip(jnp.where(lower, z - 1, z + 1), 0, nz - 1)
            pl.semaphore_wait(far_sem, 1)
            pl.semaphore_signal(far_sem, inc=1, device_id=(t, edge), device_id_type=MESH)

    with mark("e_next0"):
        chain(0, NEXT)
    chain(1, NEAR, (1,))
    with mark("e_edge"):
        @pl.when((z == 0) | (z == nz - 1))
        def _():
            pl.semaphore_wait(far_sem, 1)

    chain(0, FAR)
    chain(1, FAR)
    with mark("f_agf00"):
        ag_forward(0, 0)
    with mark("g_turn"):
        get_cot.wait()
        turned_cot = cotv[...].T
        for zz in range(nz):
            for tt in range(n):
                cott[zz * rows + tt * part : zz * rows + (tt + 1) * part, pl.ds(mine, cols)] = (
                    turned_cot[(tt * nz + zz) * part : (tt * nz + zz + 1) * part]
                )
        ag_wait(0, 0)
        normed(flip(t, 1))
    with mark("i_agf01"):
        ag_forward(0, 1)
    with mark("j_next1a"):
        chain(1, NEXT, (0,))
    with mark("k_chainend0"):
        chain_end(0)
    ag_start(2)
    with mark("l_norms"):
        normed(flip(t, 2))
        normed(flip(t, 4))
    with mark("m_next1b"):
        chain(1, NEXT, (1,))
    loaded(w1.at[own_rows, 2 * cols : 3 * cols], 3)
    chain(2, NEAR)
    chain(2, FAR)
    with mark("n_agf02"):
        ag_forward(0, 2)
    with mark("o_norms"):
        received(ag_sem(0, 7), ag_many(0, 2))
        normed(flip(t, 3))
        normed(flip(t, 5))
        normed(flip(t, 6))
    with mark("q_agf20"):
        ag_forward(2, 0)
    ag_start(1)
    with mark("p_norm"):
        received(ag_sem(0, 9), ag_many(0, 1))
        normed(flip(t, 7))
    with mark("r_chainend1"):
        chain_end(1)
    with mark("ra_next2"):
        chain(2, NEXT)
    loaded(w2.at[own_rows, :], 4)
    chain(3, NEAR)
    with mark("s_projqk"):
        for pair in range(groups):
            project(nbuf, w1, pair, (q1, k1a, k1b), None)

    length = length_ref[0]
    count = count_ref[0]
    row = lax.broadcasted_iota(jnp.int32, (fr, fr), 0)
    col = lax.broadcasted_iota(jnp.int32, (fr, fr), 1)
    low = -1e30

    def spans(b):
        first = max(b - LEFT_MAX, 0)
        return pl.ds(first * fr, (b + 1 - first) * fr), b - first

    def causal(b):
        span, before = spans(b)
        size = (before + 1) * fr
        query = q1[b * fr : (b + 1) * fr, :]
        both = dot_t(query, jnp.concatenate([k1a[span, :], k1b[span, :]], axis=0))
        spos = (b - before) * fr + lax.broadcasted_iota(jnp.int32, (1, size), 1)
        apart = before - lax.broadcasted_iota(jnp.int32, (1, size), 1) // fr
        bias = jnp.where((apart <= count) & (spos < length), 0.0, low)
        expos, inverse = [], []
        for h in range(per):
            scores = both[:, h * size : (h + 1) * size]
            now = scores[:, before * fr :]
            now = jnp.where(
                row > col,
                now + bias[:, before * fr :],
                jnp.where(row == col, now, low),
            )
            if before:
                now = jnp.concatenate(
                    [scores[:, : before * fr] + bias[:, : before * fr], now], axis=1
                )
            top = jnp.max(now, axis=-1, keepdims=True)
            expo = jnp.exp2((now - top) * scale)
            inverse.append(1.0 / jnp.sum(expo, axis=-1, keepdims=True))
            expos.append(expo.astype(jnp.bfloat16))
        p1[b, :, : per * size] = jnp.concatenate(expos, axis=1)
        r1[b] = jnp.where(col // head == 0, inverse[0], inverse[1])

    def causal_mix(b):
        span, before = spans(b)
        size = (before + 1) * fr
        mixed = dot(
            p1[b, :, : per * size], jnp.concatenate([v1a[span, :], v1b[span, :]], axis=0)
        )
        ctx1s[b * fr : (b + 1) * fr, :] = (mixed * r1[b]).astype(jnp.bfloat16)

    with mark("t_soft0"):
        causal(0)
        causal(1)
    with mark("ta_agf21"):
        ag_forward(2, 1)
    with mark("t_soft1"):
        causal(2)
        causal(3)
    with mark("td_agf22"):
        ag_forward(2, 2)
    with mark("t_soft2"):
        causal(4)
        causal(5)
        causal(6)
        causal(7)
    with mark("u_agf10"):
        ag_forward(1, 0)
    with mark("v_chainend2"):
        chain_end(2)
    chain(3, FAR)
    with mark("w_projv"):
        for pair in range(groups):
            project(nbuf, w1, pair, None, (v1a, v1b))

    def cx_copy(g, m):
        to = flip(t, (m, 4, 2)[max(m - 5, 0)])
        if m < 6:
            src = ctx1s.at[at_rows(2 * g + lax.rem(core + m, 2), fr), :]
            dst = ctxall.at[g, :, at_cols(turned(t))]
        else:
            first = turned(flip(t, 2 if m == 6 else 4) // 2 * 2)
            src = ctxall.at[
                g,
                pl.ds((m - 6) * (fr // 2), fr // 2),
                pl.ds(pl.multiple_of(first * cols, 2 * cols), 2 * cols),
            ]
            dst = src
        return pltpu.make_async_remote_copy(
            src_ref=src, dst_ref=dst,
            send_sem=CROSS, recv_sem=cx_recv.at[3 * g + (0, 2, 0, 0, 1, 1, 2, 2)[m]],
            device_id=(to, z), device_id_type=MESH,
        )

    def cx_wait(g, kind):
        received(cx_recv.at[3 * g + kind], ctxall.at[g, :, 0 : (2, 2, 3)[kind] * cols])

    def cx_forward(g):
        cx_wait(g, 0)
        cx_copy(g, 6).start()
        cx_wait(g, 1)
        cx_copy(g, 7).start()

    def cx_send(g):
        for m in (2, 4, 3, 5, 1):
            cx_copy(g, m).start()

    with mark("x_mix"):
        for g in range(groups):
            causal_mix(2 * g)
            causal_mix(2 * g + 1)
            if g < 3:
                cx_send(g)
            ctxall[g, :, at_cols(turned(t))] = ctx1s[at_rows(2 * g + core, fr), :]
    with mark("xa_agf11"):
        ag_forward(1, 1)
    with mark("xb_next3"):
        chain(3, NEXT)
    chain(4, NEAR)
    with mark("xd_fwd0"):
        cx_forward(0)
    cx_send(3)
    with mark("xc_agf12"):
        ag_forward(1, 2)
    with mark("xe_fwd1"):
        cx_forward(1)
    chain(4, FAR)
    with mark("xf_agp2"):
        ag_partner(2)

    def nx_copy(g, other):
        view = nbuf2.at[2 * g + (1 - core if other else core)]
        return pltpu.make_async_remote_copy(
            src_ref=view, dst_ref=view,
            send_sem=PAIR, recv_sem=nx_recv.at[g],
            device_id=(flip(t, 1), z), device_id_type=MESH,
        )

    def out_block(g):
        cx_wait(g, 2)
        b = 2 * g + core
        mixed = dot(ctxall[g], wo[...])
        hidden = (fbuf[b].astype(jnp.float32) + mixed).astype(jnp.bfloat16)
        nbuf2[b] = norm_rows(hidden, gains[1:2, :])
        nx_copy(g, False).start()

    tail = -(-RIGHT // 16) * 16
    wide = lax.broadcasted_iota(jnp.int32, (tail, tail), 1)
    long = lax.broadcasted_iota(jnp.int32, (tail, tail), 0) + (fr - tail)

    def ahead(b):
        query = q2[b * fr : (b + 1) * fr, :]
        here = pl.ds(b * fr, fr)
        both = dot_t(query, jnp.concatenate([k2a[here, :], k2b[here, :]], axis=0))
        seen = jnp.where(b * fr + lax.broadcasted_iota(jnp.int32, (1, fr), 1) < length, 0.0, low)
        after = None
        if b < n - 1:
            there = pl.ds((b + 1) * fr, tail)
            after = dot_t(
                query[fr - tail :], jnp.concatenate([k2a[there, :], k2b[there, :]], axis=0)
            )
            spos = (b + 1) * fr + lax.broadcasted_iota(jnp.int32, (1, tail), 1)
            late = jnp.where(spos < length, 0.0, low)
        expos, lates, inverse = [], [], []
        for h in range(per):
            now = both[:, h * fr : (h + 1) * fr]
            now = jnp.where(
                row == col, now, jnp.where(col <= row + RIGHT, now + seen, low)
            )
            top = jnp.max(now, axis=-1, keepdims=True)
            if after is not None:
                then = after[:, h * tail : (h + 1) * tail]
                then = jnp.where(wide + fr <= long + RIGHT, then + late, low)
                top = jnp.concatenate(
                    [
                        top[: fr - tail],
                        jnp.maximum(top[fr - tail :], jnp.max(then, axis=-1, keepdims=True)),
                    ],
                    axis=0,
                )
            expo = jnp.exp2((now - top) * scale)
            total = jnp.sum(expo, axis=-1, keepdims=True)
            if after is not None:
                then = jnp.exp2((then - top[fr - tail :]) * scale)
                total = jnp.concatenate(
                    [
                        total[: fr - tail],
                        total[fr - tail :] + jnp.sum(then, axis=-1, keepdims=True),
                    ],
                    axis=0,
                )
                lates.append(then.astype(jnp.bfloat16))
            inverse.append(1.0 / total)
            expos.append(expo.astype(jnp.bfloat16))
        p2[b] = jnp.concatenate(expos, axis=1)
        if after is not None:
            pn2[b] = jnp.concatenate(lates, axis=1)
        valid = b * fr + row < length
        r2[b] = jnp.where(valid, jnp.where(col // head == 0, inverse[0], inverse[1]), 0.0)

    def ahead_mix(b):
        here = pl.ds(b * fr, fr)
        mixed = dot(p2[b], jnp.concatenate([v2a[here, :], v2b[here, :]], axis=0))
        if b < n - 1:
            there = pl.ds((b + 1) * fr, tail)
            extra = dot(pn2[b], jnp.concatenate([v2a[there, :], v2b[there, :]], axis=0))
            mixed = jnp.concatenate([mixed[: fr - tail], mixed[fr - tail :] + extra], axis=0)
        ctx2s[b * fr : (b + 1) * fr, :] = (mixed * r2[b]).astype(jnp.bfloat16)

    def second(g):
        nx_copy(g, True).wait_recv()
        project(nbuf2, w2, g, (q2, k2a, k2b), None)
        if g:
            ahead(2 * g - 1)
        ahead(2 * g)

    with mark("y_out0"):
        out_block(0)
    with mark("ya_fwd2"):
        cx_forward(2)
    with mark("yb_next4"):
        chain(4, NEXT)
    with mark("y_out1"):
        out_block(1)
    with mark("yc_fwd3"):
        cx_forward(3)
    ag_start(3)
    with mark("yd_chainend3"):
        chain_end(3)
    with mark("ye_second0"):
        second(0)
    with mark("y_out2"):
        out_block(2)
    with mark("ye_second1"):
        second(1)
    with mark("y_out3"):
        out_block(3)
    with mark("yg_agf30"):
        ag_forward(3, 0)
    with mark("ye_second2"):
        second(2)
    with mark("yh_agf31"):
        ag_forward(3, 1)
    with mark("yf_agp1"):
        ag_partner(1)
    with mark("ye_second3"):
        second(3)
        ahead(n - 1)
    with mark("yk_agf32"):
        ag_forward(3, 2)
    with mark("yi_chainend4"):
        chain_end(4)
    with mark("yj_mix2"):
        for g in range(groups):
            project(nbuf2, w2, g, None, (v2a, v2b))
        for b in range(n):
            ahead_mix(b)
    with mark("yl_agp3"):
        ag_partner(3)

    def back_copy(d):
        return pltpu.make_async_remote_copy(
            src_ref=ctx2s.at[at_rows(lax.rem(t + d, n), fr), :],
            dst_ref=ctx2.at[:, at_cols(t)],
            send_sem=BACK, recv_sem=BACK_IN,
            device_id=(lax.rem(t + d, n), z), device_id_type=MESH,
        )

    edge, middle = jnp.where(lower, 0, nz - 1), jnp.where(lower, 1, nz - 2)
    far_edge, far_middle = nz - 1 - edge, nz - 1 - middle
    beside = jnp.where(inner, edge, middle)

    def term(zz):
        return dot(cott[at_rows(zz, rows), :], ctx2s[...])

    def grad_copy(index, slot, to, to_z):
        return pltpu.make_async_remote_copy(
            src_ref=gsend.at[index, at_rows(to, part), :],
            dst_ref=grecv.at[slot, :, at_cols(t)],
            send_sem=GRAD, recv_sem=GRAD_IN,
            device_id=(to, to_z), device_id_type=MESH,
        )

    def halves_of(h):
        return pl.ds(h * half, half)

    with mark("yz_back"):
        for d in range(1, n):
            back_copy(d).start()
        ctx2[:, at_cols(t)] = ctx2s[at_rows(t, fr), :]
    with mark("z_terms"):
        for index, to_z in enumerate((far_edge, far_middle)):
            value = term(to_z)
            fsum[index] = value
            gsend[index] = value.astype(jnp.bfloat16)

            @pl.when(~inner)
            def _():
                for h in range(2):
                    pltpu.make_async_remote_copy(
                        src_ref=gsend.at[index, halves_of(h), :],
                        dst_ref=pbuf.at[index, halves_of(h), :],
                        send_sem=GRAD, recv_sem=pre_sem.at[2 * index + h],
                        device_id=(t, middle), device_id_type=MESH,
                    ).start()

        gsend[2] = term(beside).astype(jnp.bfloat16)
        for d in range(n):
            grad_copy(2, 1, lax.rem(t + d, n), beside).start()
        gsend[3] = term(z).astype(jnp.bfloat16)
        for d in range(1, n):
            grad_copy(3, 0, lax.rem(t + d, n), z).start()
        grecv[0, :, at_cols(t)] = gsend[3, at_rows(t, part), :]
    with mark("za_pre"):
        @pl.when(inner)
        def _():
            for index, to_z in enumerate((far_edge, far_middle)):
                for h in range(2):
                    view = pbuf.at[index, halves_of(h), :]
                    received(pre_sem.at[2 * index + h], view)
                    gsend[index, halves_of(h), :] = (
                        fsum[index, halves_of(h), :] + view[...].astype(jnp.float32)
                    ).astype(jnp.bfloat16)
                    for d in range(n // 2):
                        grad_copy(index, 2, h * (n // 2) + lax.rem(t + d, n // 2), to_z).start()

    with mark("za_grads"):
        received(GRAD_IN, ctx2s.at[0 : (3 * n - 1) * part, :])
        total = grecv[0].astype(jnp.float32)
        for slot in (1, 2):
            total = total + grecv[slot].astype(jnp.float32)
        grad_ref[...] = total
    with mark("zb_back"):
        received(BACK_IN, ctx2.at[:, 0 : (n - 1) * cols])
        context_ref[...] = ctx2[...]
    with mark("zd_sent"):
        for which in range(4):
            ag_sent(which)
        whole = 7 * rows * cols // width

        @pl.when((z == 0) | (z == nz - 1))
        def _():
            sent(CHAIN, cott.at[0 : 2 * whole, :])

        @pl.when((z > 0) & (z < nz - 1))
        def _():
            sent(CHAIN, cott.at[0 : 4 * whole, :])

        sent(CROSS, cott.at[0 : 7 * groups * fr * cols // width, :])
        sent(PAIR, nbuf2.at[0:groups])
        sent(BACK, ctx2.at[:, 0 : (n - 1) * cols])
        sent(GRAD, ctx2s.at[0 : (n * nz - 1) * part, :])


def hand_out(context_ref, grad_ref, context_out, grad_out):
    context_out[...] = context_ref[...]
    grad_out[...] = grad_ref[...]


def by_heads(
    n, nz, frames, gain_one, qkv_one, out_one, gain_two, qkv_two, lengths, left_counts, cotangent
):
    _, fr, width = frames.shape
    cols = width // n
    rows = width // nz
    span = n * fr
    tail = -(-RIGHT // 16) * 16
    per = HEADS // n
    vmem = pl.BlockSpec(memory_space=pltpu.VMEM)
    smem = pl.BlockSpec(memory_space=pltpu.SMEM)
    hbm = pl.BlockSpec(memory_space=pltpu.HBM)
    bf16, f32 = jnp.bfloat16, jnp.float32
    dma = pltpu.SemaphoreType.DMA
    large = (
        frames[0], gain_one[None], qkv_one, out_one, gain_two[None], qkv_two, cotangent[0],
    )
    large = [pltpu.with_memory_space_constraint(value, pltpu.HBM) for value in large]
    context, grad = pl.pallas_call(
        functools.partial(heads_kernel, n, nz),
        out_shape=(
            jax.ShapeDtypeStruct((fr, width), bf16),
            jax.ShapeDtypeStruct((rows // n, width), f32),
        ),
        in_specs=[hbm] * 6 + [smem] * 2 + [hbm],
        out_specs=(vmem, vmem),
        scratch_shapes=[
            pltpu.VMEM((n, fr, width), bf16),
            pltpu.VMEM((n, fr, width), bf16),
            pltpu.VMEM((n, fr, width), bf16),
            pltpu.VMEM((width, 3 * cols), bf16),
            pltpu.VMEM((width, 3 * cols), bf16),
            pltpu.VMEM((width, width), bf16),
            pltpu.VMEM((fr, width), bf16),
            pltpu.VMEM((width, span), bf16),
            pltpu.VMEM((2, width), f32),
            *[pltpu.VMEM((span, cols), bf16)] * 5,
            pltpu.VMEM((n, fr, per * (LEFT_MAX + 1) * fr), bf16),
            pltpu.VMEM((n, fr, cols), f32),
            pltpu.VMEM((span, cols), bf16),
            pltpu.VMEM((n // 2, fr, width), bf16),
            *[pltpu.VMEM((span, cols), bf16)] * 5,
            pltpu.VMEM((n, fr, per * fr), bf16),
            pltpu.VMEM((n, tail, per * tail), bf16),
            pltpu.VMEM((n, fr, cols), f32),
            pltpu.VMEM((span, cols), bf16),
            pltpu.VMEM((fr, width), bf16),
            pltpu.VMEM((nz, rows, cols), bf16),
            pltpu.VMEM((3, rows // n, width), bf16),
            pltpu.VMEM((2, rows, cols), f32),
            pltpu.VMEM((2, rows, cols), bf16),
            dma((7,)),
            dma((4,)),
            dma((30,)),
            dma((8 * (nz - 1),)),
            dma((3 * n // 2,)),
            dma((n // 2,)),
            dma((7,)),
            pltpu.SemaphoreType.REGULAR,
            dma((4,)),
        ],
        compiler_params=pltpu.CompilerParams(
            collective_id=0, has_side_effects=True, vmem_limit_bytes=44 * 1024 * 1024
        ),
    )(*large[:6], lengths, left_counts, large[6])
    context, grad = pl.pallas_call(
        hand_out,
        out_shape=(
            jax.ShapeDtypeStruct((fr, width), bf16),
            jax.ShapeDtypeStruct((rows // n, width), f32),
        ),
        in_specs=[vmem, vmem],
        out_specs=(vmem, vmem),
        compiler_params=pltpu.CompilerParams(vmem_limit_bytes=4 * 1024 * 1024),
    )(context, grad)
    return (context[None], grad)


def solution(mesh):
    n_tm = mesh.shape["tm"]
    even = n_tm == 2 * CHIPS and mesh.shape["fsdp"] == CHIPS and HEADS == 2 * n_tm
    chosen = functools.partial(by_heads, n_tm, mesh.shape["fsdp"]) if even else on_device
    in_specs = (
        P("fsdp", "tm", None),
        P(),
        P("fsdp", None),
        P("fsdp", None),
        P(),
        P("fsdp", None),
        P("fsdp"),
        P("fsdp"),
        P("fsdp", "tm", None),
    )
    out_specs = (P("fsdp", "tm", None), P(("tm", "fsdp"), None))
    return jax.shard_map(
        chosen, mesh=mesh, in_specs=in_specs, out_specs=out_specs, check_vma=False
    )
```

```python
import contextlib
import functools
import math

import jax
import jax.numpy as jnp
from jax import lax
from jax.experimental import pallas as pl
from jax.experimental.pallas import tpu as pltpu
from jax.sharding import PartitionSpec as P

HEADS = 16
LEFT_MAX = 2
RIGHT = 23
CHIPS = 4
SCOPES = False


def mark(name):
    return jax.named_scope(name) if SCOPES else contextlib.nullcontext()


def from_behind(block, axis, distance):
    devices = range(lax.axis_size(axis))
    route = [(i - distance, i) for i in devices if i - distance in devices]
    return lax.ppermute(block, axis, route)


def norm_rows(values, gain):
    wide = values.astype(jnp.float32)
    mean = jnp.mean(wide, axis=-1, keepdims=True)
    var = jnp.mean((wide - mean) ** 2, axis=-1, keepdims=True)
    return ((wide - mean) * lax.rsqrt(var + 1e-05) * gain).astype(jnp.bfloat16)


def attend(query, keys, values, allowed, heads):
    rows_q, width = query.shape
    head = width // heads
    scale = 1.0 / head**0.5
    q_heads = query.reshape(rows_q, heads, head)
    k_heads = keys.reshape(keys.shape[0], heads, head)
    v_heads = values.reshape(values.shape[0], heads, head)
    scores = (
        jnp.einsum("qhe,khe->hqk", q_heads, k_heads, preferred_element_type=jnp.float32) * scale
    )
    scores = jnp.where(allowed[None], scores, -1e30)
    top = jnp.max(scores, axis=-1, keepdims=True)
    expo = jnp.exp(scores - top)
    weights = (expo / jnp.sum(expo, axis=-1, keepdims=True)).astype(jnp.bfloat16)
    ctx = jnp.einsum("hqk,khe->qhe", weights, v_heads, preferred_element_type=jnp.float32)
    return ctx.reshape(rows_q, width).astype(jnp.bfloat16)


def add_rows(left, piece):
    return jnp.dot(left, piece, preferred_element_type=jnp.float32)


def on_device(
    frames, gain_one, qkv_one, out_one, gain_two, qkv_two, lengths, left_counts, cotangent
):
    local = frames[0]
    grad_in = cotangent[0]
    fr, width = local.shape
    block = lax.axis_index("tm")
    length = lengths[0]
    count = left_counts[0]
    norm_one = norm_rows(local, gain_one)
    proj = add_rows(norm_one, lax.all_gather(qkv_one, "fsdp", axis=0, tiled=True))
    proj = proj.astype(jnp.bfloat16)
    query = proj[:, :width]
    key_value = proj[:, width:]
    earlier = [from_behind(key_value, "tm", step) for step in range(LEFT_MAX, 0, -1)]
    gathered = jnp.concatenate(earlier + [key_value], axis=0)
    rows = jnp.arange(fr, dtype=jnp.int32)
    cols = jnp.arange((LEFT_MAX + 1) * fr, dtype=jnp.int32)
    tpos = block * fr + rows[:, None]
    spos = (block - LEFT_MAX) * fr + cols[None, :]
    apart = LEFT_MAX - cols[None, :] // fr
    allowed = (spos >= 0) & (spos <= tpos) & (apart <= count) & ((spos < length) | (spos == tpos))
    ctx_one = attend(query, gathered[:, :width], gathered[:, width:], allowed, HEADS)
    out_proj = add_rows(ctx_one, lax.all_gather(out_one, "fsdp", axis=0, tiled=True))
    hidden = (local.astype(jnp.float32) + out_proj).astype(jnp.bfloat16)
    norm_two = norm_rows(hidden, gain_two)
    proj2 = add_rows(norm_two, lax.all_gather(qkv_two, "fsdp", axis=0, tiled=True))
    proj2 = proj2.astype(jnp.bfloat16)
    query2 = proj2[:, :width]
    key_value2 = proj2[:, width:]
    ahead = from_behind(key_value2[:RIGHT], "tm", -1)
    joined = jnp.concatenate([key_value2, ahead], axis=0)
    cols2 = jnp.arange(fr + RIGHT, dtype=jnp.int32)
    spos2 = block * fr + cols2[None, :]
    allowed2 = (cols2[None, :] <= rows[:, None] + RIGHT) & ((spos2 < length) | (spos2 == tpos))
    ctx_two = attend(query2, joined[:, :width], joined[:, width:], allowed2, HEADS)
    valid = block * fr + rows < length
    context = jnp.where(valid[:, None], ctx_two, jnp.zeros_like(ctx_two))
    weight_grad = lax.psum_scatter(
        lax.dot_general(
            grad_in, context, (((0,), (0,)), ((), ())), preferred_element_type=jnp.float32
        ),
        ("tm", "fsdp"),
        scatter_dimension=0,
        tiled=True,
    )
    return (context[None], weight_grad)


MESH = pl.DeviceIdType.MESH


def flip(index, mask):
    out, bit = index, 1
    while bit <= mask:
        if mask & bit:
            out = out + bit * (1 - 2 * ((index // bit) % 2))
        bit *= 2
    return out


def heads_kernel(
    n,
    nz,
    frames_ref, gain_one_ref, qkv_one_ref, out_one_ref, gain_two_ref, qkv_two_ref,
    length_ref, count_ref, cot_ref,
    context_ref, grad_ref,
    fbuf, nbuf, nbuf2, w1, w2, wo, cotv, cott, gains,
    q1, k1a, k1b, v1a, v1b, p1, r1, ctx1s, ctxall,
    q2, k2a, k2b, v2a, v2b, p2, pn2, r2, ctx2s, ctx2,
    gsend, grecv, fsum, pbuf,
    local_sem, ag_send, ag_recv, ch_recv, cx_recv, nx_recv, one_sem, far_sem, pre_sem,
):
    t = lax.axis_index("tm")
    z = lax.axis_index("fsdp")
    fr, width = frames_ref.shape
    cols = width // n
    head = width // HEADS
    per = HEADS // n
    rows = width // nz
    part = rows // n
    groups = n // 2
    scale = math.log2(math.e) / head**0.5
    mine = pl.multiple_of(t * cols, cols)
    core = lax.rem(t, 2)

    def at_cols(index):
        return pl.ds(pl.multiple_of(index * cols, cols), cols)

    def at_rows(index, size):
        return pl.ds(pl.multiple_of(index * size, size), size)

    barrier = pltpu.get_barrier_semaphore()
    for mask in (4, 2, 1):
        pl.semaphore_signal(barrier, inc=1, device_id=(flip(t, mask), z), device_id_type=MESH)

    @pl.when(z > 0)
    def _():
        pl.semaphore_signal(barrier, inc=1, device_id=(t, z - 1), device_id_type=MESH)

    @pl.when(z < nz - 1)
    def _():
        pl.semaphore_signal(barrier, inc=1, device_id=(t, z + 1), device_id_type=MESH)

    own_rows = at_rows(z, rows)

    def load(src, dst, index):
        return pltpu.make_async_copy(src, dst, local_sem.at[index])

    def load_cols(src, dst, j, index):
        return load(
            src.at[:, pl.ds(pl.multiple_of(j * width + mine, cols), cols)],
            dst.at[own_rows, pl.ds(j * cols, cols)],
            index,
        )

    get_frames = load(frames_ref, fbuf.at[t], 0)
    get_wo = load(out_one_ref, wo.at[pl.ds(0, rows), :], 1)
    get_w1 = [load_cols(qkv_one_ref, w1, j, 2 + j // 2) for j in range(3)]
    get_w2 = [load_cols(qkv_two_ref, w2, j, 4) for j in range(3)]
    get_cot = load(cot_ref, cotv, 5)
    get_gains = [load(gain_one_ref, gains.at[0:1], 6), load(gain_two_ref, gains.at[1:2], 6)]
    for copy in [get_frames, get_wo, *get_w1, *get_gains, get_cot, *get_w2]:
        copy.start()

    def loaded(view, index):
        load(view, view, index).wait()

    CHAIN, CROSS, PAIR, BACK, GRAD, BACK_IN, GRAD_IN = (one_sem.at[i] for i in range(7))

    def sent(sem, view):
        pltpu.make_async_remote_copy(
            src_ref=view, dst_ref=view, send_sem=sem, recv_sem=sem,
            device_id=(flip(t, 1), z), device_id_type=MESH,
        ).wait_send()

    def received(sem, view):
        pltpu.make_async_remote_copy(
            src_ref=view, dst_ref=view, send_sem=sem, recv_sem=sem,
            device_id=(flip(t, 1), z), device_id_type=MESH,
        ).wait_recv()

    half = rows // 2

    NEAR, NEXT, FAR = 0, 1, 2

    def chain_view(which, shard, h, at):
        place = lax.rem(shard - at + nz, nz) if which == 0 else shard
        if h is None:
            span = at_rows(place, rows)
        else:
            span = pl.ds(pl.multiple_of(place * rows + h * half, half), half)
        if which == 0:
            return wo.at[span, pl.ds(mine, cols)]
        wide = pl.ds(0, 2 * cols) if which in (1, 3) else pl.ds(2 * cols, cols)
        return (w1 if which < 3 else w2).at[span, wide]

    def chain_sem(which, shard, h, at):
        apart = lax.rem(shard - at + nz, nz) - 1
        if h is None:
            return ch_recv.at[6 * (nz - 1) + (which - 3) * (nz - 1) + apart]
        return ch_recv.at[(2 * which + h) * (nz - 1) + apart]

    def pieces(which):
        return (0, 1) if which < 3 else (None,)

    def chain_cond(kind, up):
        if kind == NEAR:
            return z < nz - 1 if up else z > 0
        if kind == NEXT:
            return (z > 0) & (z < nz - 1)
        return z == 0 if up else z == nz - 1

    def chain_wait(which, shard, h):
        received(chain_sem(which, shard, h, z), chain_view(which, shard, h, z))

    def chain(which, kind, halves=None):
        for h in halves or pieces(which):
            for up in (True, False):
                @pl.when(chain_cond(kind, up))
                def _():
                    way = 1 if up else -1
                    shard = z - way if kind == NEXT else z
                    to = (nz - 1 if up else 0) if kind == FAR else z + way
                    shard, to = jnp.clip(shard, 0, nz - 1), jnp.clip(to, 0, nz - 1)
                    if kind == NEXT:
                        chain_wait(which, shard, h)
                    pltpu.make_async_remote_copy(
                        src_ref=chain_view(which, shard, h, z),
                        dst_ref=chain_view(which, shard, h, to),
                        send_sem=CHAIN,
                        recv_sem=chain_sem(which, shard, h, to),
                        device_id=(t, to),
                        device_id_type=MESH,
                    ).start()

    def chain_end(which):
        for apart in range(1, nz):
            for way in (1, -1):
                ends = (z == nz - 1) if way == 1 else (z == 0)
                there = z - way * apart
                inside = (there >= 0) & (there < nz)
                @pl.when(inside & ends if apart == 1 else inside)
                def _():
                    for h in pieces(which):
                        chain_wait(which, jnp.clip(there, 0, nz - 1), h)

    early = width * 3 // 8

    def ag_view(which, index, piece):
        if which == 0:
            if piece is None:
                return fbuf.at[index]
            return fbuf.at[index, pl.ds(piece * (fr // 2), fr // 2), :]
        buf, first, size = (
            None, (cott, 0, early), (wo, rows, width - rows), (cott, early, width - early),
        )[which]
        if piece is None:
            return buf.at[pl.ds(first, size), at_cols(index)]
        return buf.at[pl.ds(first + piece * (size // 2), size // 2), at_cols(index)]

    slots = (
        (0, None, 1), (0, 0, 2), (0, 1, 2), (0, 1, 4), (0, 0, 4),
        (2, 0, 4), (4, 1, 2),
        (2, None, 1), (4, None, 1), (6, 0, 1), (6, 1, 1),
    )

    shared = {1: 0, 3: 1, 2: 2, 4: 3, 5: 4, 6: 5, 0: 6}

    def ag_sem(which, slot):
        if which == 0:
            return ag_recv.at[shared.get(slot, 7 if slot < 9 else 8)]
        return ag_recv.at[9 + 7 * (which - 1) + shared.get(slot, 6)]

    def ag_copy(which, slot):
        block, piece, to = slots[slot]
        view = ag_view(which, flip(t, block), piece)
        return pltpu.make_async_remote_copy(
            src_ref=view, dst_ref=view,
            send_sem=ag_send.at[which], recv_sem=ag_sem(which, slot),
            device_id=(flip(t, to), z), device_id_type=MESH,
        )

    def ag_wait(which, slot):
        block, piece, to = slots[slot]
        received(ag_sem(which, slot), ag_view(which, flip(t, block ^ to), piece))

    def ag_start(which):
        for slot in (1, 3, 2, 4, 0):
            ag_copy(which, slot).start()

    def ag_forward(which, stage):
        for waits, slot in (
            (((1, 5), (3, 6)), ((2, 7), (4, 8)), ((5, 9), (6, 10)))[stage]
        ):
            ag_wait(which, waits)
            ag_copy(which, slot).start()

    def ag_many(which, blocks):
        if which == 0:
            return fbuf.at[0:blocks]
        first = (0, 0, rows, early)[which]
        size = (0, early, width - rows, width - early)[which]
        return (wo if which == 2 else cott).at[first : first + size, 0 : blocks * cols]

    def ag_partner(which):
        received(ag_sem(which, 0), ag_many(which, 4))

    def ag_sent(which):
        sent(ag_send.at[which], ag_many(which, n - 1))

    def normed(index):
        nbuf[index] = norm_rows(fbuf[index], gains[0:1, :])

    def masked_heads(values):
        lane = lax.broadcasted_iota(jnp.int32, values.shape, 1) // head
        blank = jnp.zeros_like(values)
        return jnp.where(lane == 0, values, blank), jnp.where(lane == 1, values, blank)

    def dot(left, right):
        return jnp.dot(left, right, preferred_element_type=jnp.float32)

    def dot_t(left, right):
        return lax.dot_general(
            left, right, (((1,), (1,)), ((), ())), preferred_element_type=jnp.float32
        )

    def project(buf, weight, pair, targets_qk, targets_v):
        left = buf[2 * pair : 2 * pair + 2].reshape(2 * fr, width)
        span = pl.ds(2 * pair * fr, 2 * fr)
        if targets_qk is not None:
            q, ka, kb = targets_qk
            out = dot(left, weight[:, : 2 * cols]).astype(jnp.bfloat16)
            q[span, :] = out[:, :cols]
            ka[span, :], kb[span, :] = masked_heads(out[:, cols:])
        else:
            va, vb = targets_v
            out = dot(left, weight[:, 2 * cols :]).astype(jnp.bfloat16)
            va[span, :], vb[span, :] = masked_heads(out)

    def turned(index):
        return lax.rem(index - z * (rows // cols) + n, n)

    with mark("a_barrier"):
        pl.semaphore_wait(
            barrier, 3 + jnp.where(z > 0, 1, 0) + jnp.where(z < nz - 1, 1, 0)
        )
    with mark("b_frames"):
        get_frames.wait()
    ag_start(0)
    get_wo.wait()
    chain(0, NEAR)
    inner = (z > 0) & (z < nz - 1)
    lower = z < nz // 2

    @pl.when(inner)
    def _():
        other = jnp.clip(jnp.where(lower, z + 1, z - 1), 0, nz - 1)
        pl.semaphore_signal(far_sem, inc=1, device_id=(t, other), device_id_type=MESH)

    loaded(w1.at[own_rows, 0 : 2 * cols], 2)
    chain(1, NEAR, (0,))
    with mark("d_norm"):
        loaded(gains, 6)
        normed(t)
    with mark("e_far"):
        @pl.when(inner)
        def _():
            edge = jnp.clip(jnp.where(lower, z - 1, z + 1), 0, nz - 1)
            pl.semaphore_wait(far_sem, 1)
            pl.semaphore_signal(far_sem, inc=1, device_id=(t, edge), device_id_type=MESH)

    with mark("e_next0"):
        chain(0, NEXT)
    chain(1, NEAR, (1,))
    with mark("e_edge"):
        @pl.when((z == 0) | (z == nz - 1))
        def _():
            pl.semaphore_wait(far_sem, 1)

    chain(0, FAR)
    chain(1, FAR)
    with mark("f_agf00"):
        ag_forward(0, 0)
    with mark("g_turn"):
        get_cot.wait()
        turned_cot = cotv[...].T
        for zz in range(nz):
            for tt in range(n):
                cott[zz * rows + tt * part : zz * rows + (tt + 1) * part, pl.ds(mine, cols)] = (
                    turned_cot[(tt * nz + zz) * part : (tt * nz + zz + 1) * part]
                )
        ag_wait(0, 0)
        normed(flip(t, 1))
    with mark("i_agf01"):
        ag_forward(0, 1)
    with mark("j_next1a"):
        chain(1, NEXT, (0,))
    with mark("k_chainend0"):
        chain_end(0)
    ag_start(2)
    with mark("l_norms"):
        normed(flip(t, 2))
        normed(flip(t, 4))
    with mark("m_next1b"):
        chain(1, NEXT, (1,))
    loaded(w1.at[own_rows, 2 * cols : 3 * cols], 3)
    chain(2, NEAR)
    chain(2, FAR)
    with mark("n_agf02"):
        ag_forward(0, 2)
    with mark("o_norms"):
        received(ag_sem(0, 7), ag_many(0, 2))
        normed(flip(t, 3))
        normed(flip(t, 5))
        normed(flip(t, 6))
    with mark("q_agf20"):
        ag_forward(2, 0)
    ag_start(1)
    with mark("p_norm"):
        received(ag_sem(0, 9), ag_many(0, 1))
        normed(flip(t, 7))
    with mark("r_chainend1"):
        chain_end(1)
    with mark("ra_next2"):
        chain(2, NEXT)
    loaded(w2.at[own_rows, :], 4)
    chain(3, NEAR)
    with mark("s_projqk"):
        for pair in range(groups):
            project(nbuf, w1, pair, (q1, k1a, k1b), None)

    length = length_ref[0]
    count = count_ref[0]
    row = lax.broadcasted_iota(jnp.int32, (fr, fr), 0)
    col = lax.broadcasted_iota(jnp.int32, (fr, fr), 1)
    low = -1e30

    def spans(b):
        first = max(b - LEFT_MAX, 0)
        return pl.ds(first * fr, (b + 1 - first) * fr), b - first

    def causal(b):
        span, before = spans(b)
        size = (before + 1) * fr
        query = q1[b * fr : (b + 1) * fr, :]
        both = dot_t(query, jnp.concatenate([k1a[span, :], k1b[span, :]], axis=0))
        spos = (b - before) * fr + lax.broadcasted_iota(jnp.int32, (1, size), 1)
        apart = before - lax.broadcasted_iota(jnp.int32, (1, size), 1) // fr
        bias = jnp.where((apart <= count) & (spos < length), 0.0, low)
        expos, inverse = [], []
        for h in range(per):
            scores = both[:, h * size : (h + 1) * size]
            now = scores[:, before * fr :]
            now = jnp.where(
                row > col,
                now + bias[:, before * fr :],
                jnp.where(row == col, now, low),
            )
            if before:
                now = jnp.concatenate(
                    [scores[:, : before * fr] + bias[:, : before * fr], now], axis=1
                )
            top = jnp.max(now, axis=-1, keepdims=True)
            expo = jnp.exp2((now - top) * scale)
            inverse.append(1.0 / jnp.sum(expo, axis=-1, keepdims=True))
            expos.append(expo.astype(jnp.bfloat16))
        p1[b, :, : per * size] = jnp.concatenate(expos, axis=1)
        r1[b] = jnp.where(col // head == 0, inverse[0], inverse[1])

    def causal_mix(b):
        span, before = spans(b)
        size = (before + 1) * fr
        mixed = dot(
            p1[b, :, : per * size], jnp.concatenate([v1a[span, :], v1b[span, :]], axis=0)
        )
        ctx1s[b * fr : (b + 1) * fr, :] = (mixed * r1[b]).astype(jnp.bfloat16)

    with mark("t_soft0"):
        causal(0)
        causal(1)
    with mark("ta_agf21"):
        ag_forward(2, 1)
    with mark("t_soft1"):
        causal(2)
        causal(3)
    with mark("td_agf22"):
        ag_forward(2, 2)
    with mark("t_soft2"):
        causal(4)
        causal(5)
        causal(6)
        causal(7)
    with mark("u_agf10"):
        ag_forward(1, 0)
    with mark("v_chainend2"):
        chain_end(2)
    chain(3, FAR)
    def cx_copy(g, m):
        to = flip(t, (m, 4, 2)[max(m - 5, 0)])
        if m < 6:
            src = ctx1s.at[at_rows(2 * g + lax.rem(core + m, 2), fr), :]
            dst = ctxall.at[g, :, at_cols(turned(t))]
        else:
            first = turned(flip(t, 2 if m == 6 else 4) // 2 * 2)
            src = ctxall.at[
                g,
                pl.ds((m - 6) * (fr // 2), fr // 2),
                pl.ds(pl.multiple_of(first * cols, 2 * cols), 2 * cols),
            ]
            dst = src
        return pltpu.make_async_remote_copy(
            src_ref=src, dst_ref=dst,
            send_sem=CROSS, recv_sem=cx_recv.at[3 * g + (0, 2, 0, 0, 1, 1, 2, 2)[m]],
            device_id=(to, z), device_id_type=MESH,
        )

    def cx_wait(g, kind):
        received(cx_recv.at[3 * g + kind], ctxall.at[g, :, 0 : (2, 2, 3)[kind] * cols])

    def cx_forward(g):
        cx_wait(g, 0)
        cx_copy(g, 6).start()
        cx_wait(g, 1)
        cx_copy(g, 7).start()

    def cx_send(g):
        for m in (2, 4, 3, 5, 1):
            cx_copy(g, m).start()

    with mark("x_mix"):
        for g in range(groups):
            project(nbuf, w1, g, None, (v1a, v1b))
            causal_mix(2 * g)
            causal_mix(2 * g + 1)
            if g < 3:
                cx_send(g)
            ctxall[g, :, at_cols(turned(t))] = ctx1s[at_rows(2 * g + core, fr), :]
    with mark("xa_agf11"):
        ag_forward(1, 1)
    with mark("xb_next3"):
        chain(3, NEXT)
    chain(4, NEAR)
    with mark("xd_fwd0"):
        cx_forward(0)
    cx_send(3)
    with mark("xc_agf12"):
        ag_forward(1, 2)
    with mark("xe_fwd1"):
        cx_forward(1)
    chain(4, FAR)
    with mark("xf_agp2"):
        ag_partner(2)

    def nx_copy(g, other):
        view = nbuf2.at[2 * g + (1 - core if other else core)]
        return pltpu.make_async_remote_copy(
            src_ref=view, dst_ref=view,
            send_sem=PAIR, recv_sem=nx_recv.at[g],
            device_id=(flip(t, 1), z), device_id_type=MESH,
        )

    def out_block(g):
        cx_wait(g, 2)
        b = 2 * g + core
        mixed = dot(ctxall[g], wo[...])
        hidden = (fbuf[b].astype(jnp.float32) + mixed).astype(jnp.bfloat16)
        nbuf2[b] = norm_rows(hidden, gains[1:2, :])
        nx_copy(g, False).start()

    tail = -(-RIGHT // 16) * 16
    wide = lax.broadcasted_iota(jnp.int32, (tail, tail), 1)
    long = lax.broadcasted_iota(jnp.int32, (tail, tail), 0) + (fr - tail)

    def ahead(b):
        query = q2[b * fr : (b + 1) * fr, :]
        here = pl.ds(b * fr, fr)
        both = dot_t(query, jnp.concatenate([k2a[here, :], k2b[here, :]], axis=0))
        seen = jnp.where(b * fr + lax.broadcasted_iota(jnp.int32, (1, fr), 1) < length, 0.0, low)
        after = None
        if b < n - 1:
            there = pl.ds((b + 1) * fr, tail)
            after = dot_t(
                query[fr - tail :], jnp.concatenate([k2a[there, :], k2b[there, :]], axis=0)
            )
            spos = (b + 1) * fr + lax.broadcasted_iota(jnp.int32, (1, tail), 1)
            late = jnp.where(spos < length, 0.0, low)
        expos, lates, inverse = [], [], []
        for h in range(per):
            now = both[:, h * fr : (h + 1) * fr]
            now = jnp.where(
                row == col, now, jnp.where(col <= row + RIGHT, now + seen, low)
            )
            top = jnp.max(now, axis=-1, keepdims=True)
            if after is not None:
                then = after[:, h * tail : (h + 1) * tail]
                then = jnp.where(wide + fr <= long + RIGHT, then + late, low)
                top = jnp.concatenate(
                    [
                        top[: fr - tail],
                        jnp.maximum(top[fr - tail :], jnp.max(then, axis=-1, keepdims=True)),
                    ],
                    axis=0,
                )
            expo = jnp.exp2((now - top) * scale)
            total = jnp.sum(expo, axis=-1, keepdims=True)
            if after is not None:
                then = jnp.exp2((then - top[fr - tail :]) * scale)
                total = jnp.concatenate(
                    [
                        total[: fr - tail],
                        total[fr - tail :] + jnp.sum(then, axis=-1, keepdims=True),
                    ],
                    axis=0,
                )
                lates.append(then.astype(jnp.bfloat16))
            inverse.append(1.0 / total)
            expos.append(expo.astype(jnp.bfloat16))
        p2[b] = jnp.concatenate(expos, axis=1)
        if after is not None:
            pn2[b] = jnp.concatenate(lates, axis=1)
        valid = b * fr + row < length
        r2[b] = jnp.where(valid, jnp.where(col // head == 0, inverse[0], inverse[1]), 0.0)

    def ahead_mix(b):
        here = pl.ds(b * fr, fr)
        mixed = dot(p2[b], jnp.concatenate([v2a[here, :], v2b[here, :]], axis=0))
        if b < n - 1:
            there = pl.ds((b + 1) * fr, tail)
            extra = dot(pn2[b], jnp.concatenate([v2a[there, :], v2b[there, :]], axis=0))
            mixed = jnp.concatenate([mixed[: fr - tail], mixed[fr - tail :] + extra], axis=0)
        ctx2s[b * fr : (b + 1) * fr, :] = (mixed * r2[b]).astype(jnp.bfloat16)

    def second(g):
        nx_copy(g, True).wait_recv()
        project(nbuf2, w2, g, (q2, k2a, k2b), None)
        if g:
            ahead(2 * g - 1)
        ahead(2 * g)

    with mark("y_out0"):
        out_block(0)
    with mark("ya_fwd2"):
        cx_forward(2)
    with mark("yb_next4"):
        chain(4, NEXT)
    with mark("y_out1"):
        out_block(1)
    with mark("yc_fwd3"):
        cx_forward(3)
    ag_start(3)
    with mark("yd_chainend3"):
        chain_end(3)
    with mark("ye_second0"):
        second(0)
    with mark("y_out2"):
        out_block(2)
    with mark("ye_second1"):
        second(1)
    with mark("y_out3"):
        out_block(3)
    with mark("yg_agf30"):
        ag_forward(3, 0)
    with mark("ye_second2"):
        second(2)
    with mark("yh_agf31"):
        ag_forward(3, 1)
    with mark("yi_chainend4"):
        chain_end(4)
    with mark("yi_projv"):
        for g in range(groups - 1):
            project(nbuf2, w2, g, None, (v2a, v2b))
    with mark("yf_agp1"):
        ag_partner(1)
    with mark("ye_second3"):
        second(3)
        ahead(n - 1)
    with mark("yk_agf32"):
        ag_forward(3, 2)
    with mark("yj_mix2"):
        project(nbuf2, w2, groups - 1, None, (v2a, v2b))
        for b in range(n):
            ahead_mix(b)
    with mark("yl_agp3"):
        ag_partner(3)

    def back_copy(d):
        return pltpu.make_async_remote_copy(
            src_ref=ctx2s.at[at_rows(lax.rem(t + d, n), fr), :],
            dst_ref=ctx2.at[:, at_cols(t)],
            send_sem=BACK, recv_sem=BACK_IN,
            device_id=(lax.rem(t + d, n), z), device_id_type=MESH,
        )

    edge, middle = jnp.where(lower, 0, nz - 1), jnp.where(lower, 1, nz - 2)
    far_edge, far_middle = nz - 1 - edge, nz - 1 - middle
    beside = jnp.where(inner, edge, middle)

    def term(zz):
        return dot(cott[at_rows(zz, rows), :], ctx2s[...])

    def grad_copy(index, slot, to, to_z):
        return pltpu.make_async_remote_copy(
            src_ref=gsend.at[index, at_rows(to, part), :],
            dst_ref=grecv.at[slot, :, at_cols(t)],
            send_sem=GRAD, recv_sem=GRAD_IN,
            device_id=(to, to_z), device_id_type=MESH,
        )

    def halves_of(h):
        return pl.ds(h * half, half)

    with mark("yz_back"):
        for d in range(1, n):
            back_copy(d).start()
        ctx2[:, at_cols(t)] = ctx2s[at_rows(t, fr), :]
    with mark("z_terms"):
        for index, to_z in enumerate((far_edge, far_middle)):
            value = term(to_z)
            fsum[index] = value
            gsend[index] = value.astype(jnp.bfloat16)

            @pl.when(~inner)
            def _():
                for h in range(2):
                    pltpu.make_async_remote_copy(
                        src_ref=gsend.at[index, halves_of(h), :],
                        dst_ref=pbuf.at[index, halves_of(h), :],
                        send_sem=GRAD, recv_sem=pre_sem.at[2 * index + h],
                        device_id=(t, middle), device_id_type=MESH,
                    ).start()

        gsend[2] = term(beside).astype(jnp.bfloat16)
        for d in range(n):
            grad_copy(2, 1, lax.rem(t + d, n), beside).start()
        gsend[3] = term(z).astype(jnp.bfloat16)
        for d in range(1, n):
            grad_copy(3, 0, lax.rem(t + d, n), z).start()
        grecv[0, :, at_cols(t)] = gsend[3, at_rows(t, part), :]
    with mark("za_pre"):
        @pl.when(inner)
        def _():
            for index, to_z in enumerate((far_edge, far_middle)):
                for h in range(2):
                    view = pbuf.at[index, halves_of(h), :]
                    received(pre_sem.at[2 * index + h], view)
                    gsend[index, halves_of(h), :] = (
                        fsum[index, halves_of(h), :] + view[...].astype(jnp.float32)
                    ).astype(jnp.bfloat16)
                    for d in range(n // 2):
                        grad_copy(index, 2, h * (n // 2) + lax.rem(t + d, n // 2), to_z).start()

    with mark("za_grads"):
        received(GRAD_IN, ctx2s.at[0 : (3 * n - 1) * part, :])
        total = grecv[0].astype(jnp.float32)
        for slot in (1, 2):
            total = total + grecv[slot].astype(jnp.float32)
        grad_ref[...] = total
    with mark("zb_back"):
        received(BACK_IN, ctx2.at[:, 0 : (n - 1) * cols])
        context_ref[...] = ctx2[...]
    with mark("zd_sent"):
        for which in range(4):
            ag_sent(which)
        whole = 7 * rows * cols // width

        @pl.when((z == 0) | (z == nz - 1))
        def _():
            sent(CHAIN, cott.at[0 : 2 * whole, :])

        @pl.when((z > 0) & (z < nz - 1))
        def _():
            sent(CHAIN, cott.at[0 : 4 * whole, :])

        sent(CROSS, cott.at[0 : 7 * groups * fr * cols // width, :])
        sent(PAIR, nbuf2.at[0:groups])
        sent(BACK, ctx2.at[:, 0 : (n - 1) * cols])
        sent(GRAD, ctx2s.at[0 : (n * nz - 1) * part, :])


def hand_out(context_ref, grad_ref, context_out, grad_out):
    context_out[...] = context_ref[...]
    grad_out[...] = grad_ref[...]


def by_heads(
    n, nz, frames, gain_one, qkv_one, out_one, gain_two, qkv_two, lengths, left_counts, cotangent
):
    _, fr, width = frames.shape
    cols = width // n
    rows = width // nz
    span = n * fr
    tail = -(-RIGHT // 16) * 16
    per = HEADS // n
    vmem = pl.BlockSpec(memory_space=pltpu.VMEM)
    smem = pl.BlockSpec(memory_space=pltpu.SMEM)
    hbm = pl.BlockSpec(memory_space=pltpu.HBM)
    bf16, f32 = jnp.bfloat16, jnp.float32
    dma = pltpu.SemaphoreType.DMA
    large = (
        frames[0], gain_one[None], qkv_one, out_one, gain_two[None], qkv_two, cotangent[0],
    )
    large = [pltpu.with_memory_space_constraint(value, pltpu.HBM) for value in large]
    context, grad = pl.pallas_call(
        functools.partial(heads_kernel, n, nz),
        out_shape=(
            jax.ShapeDtypeStruct((fr, width), bf16),
            jax.ShapeDtypeStruct((rows // n, width), f32),
        ),
        in_specs=[hbm] * 6 + [smem] * 2 + [hbm],
        out_specs=(vmem, vmem),
        scratch_shapes=[
            pltpu.VMEM((n, fr, width), bf16),
            pltpu.VMEM((n, fr, width), bf16),
            pltpu.VMEM((n, fr, width), bf16),
            pltpu.VMEM((width, 3 * cols), bf16),
            pltpu.VMEM((width, 3 * cols), bf16),
            pltpu.VMEM((width, width), bf16),
            pltpu.VMEM((fr, width), bf16),
            pltpu.VMEM((width, span), bf16),
            pltpu.VMEM((2, width), f32),
            *[pltpu.VMEM((span, cols), bf16)] * 5,
            pltpu.VMEM((n, fr, per * (LEFT_MAX + 1) * fr), bf16),
            pltpu.VMEM((n, fr, cols), f32),
            pltpu.VMEM((span, cols), bf16),
            pltpu.VMEM((n // 2, fr, width), bf16),
            *[pltpu.VMEM((span, cols), bf16)] * 5,
            pltpu.VMEM((n, fr, per * fr), bf16),
            pltpu.VMEM((n, tail, per * tail), bf16),
            pltpu.VMEM((n, fr, cols), f32),
            pltpu.VMEM((span, cols), bf16),
            pltpu.VMEM((fr, width), bf16),
            pltpu.VMEM((nz, rows, cols), bf16),
            pltpu.VMEM((3, rows // n, width), bf16),
            pltpu.VMEM((2, rows, cols), f32),
            pltpu.VMEM((2, rows, cols), bf16),
            dma((7,)),
            dma((4,)),
            dma((30,)),
            dma((8 * (nz - 1),)),
            dma((3 * n // 2,)),
            dma((n // 2,)),
            dma((7,)),
            pltpu.SemaphoreType.REGULAR,
            dma((4,)),
        ],
        compiler_params=pltpu.CompilerParams(
            collective_id=0, has_side_effects=True, vmem_limit_bytes=44 * 1024 * 1024
        ),
    )(*large[:6], lengths, left_counts, large[6])
    context, grad = pl.pallas_call(
        hand_out,
        out_shape=(
            jax.ShapeDtypeStruct((fr, width), bf16),
            jax.ShapeDtypeStruct((rows // n, width), f32),
        ),
        in_specs=[vmem, vmem],
        out_specs=(vmem, vmem),
        compiler_params=pltpu.CompilerParams(vmem_limit_bytes=4 * 1024 * 1024),
    )(context, grad)
    return (context[None], grad)


def solution(mesh):
    n_tm = mesh.shape["tm"]
    even = n_tm == 2 * CHIPS and mesh.shape["fsdp"] == CHIPS and HEADS == 2 * n_tm
    chosen = functools.partial(by_heads, n_tm, mesh.shape["fsdp"]) if even else on_device
    in_specs = (
        P("fsdp", "tm", None),
        P(),
        P("fsdp", None),
        P("fsdp", None),
        P(),
        P("fsdp", None),
        P("fsdp"),
        P("fsdp"),
        P("fsdp", "tm", None),
    )
    out_specs = (P("fsdp", "tm", None), P(("tm", "fsdp"), None))
    return jax.shard_map(
        chosen, mesh=mesh, in_specs=in_specs, out_specs=out_specs, check_vma=False
    )
```
